128 devices in a mesh: group: 8 (over z, core), pair: 16 (over y, x).
Axes of the slice: x: 4, y: 4, z: 4, core: 2. Of those that a mesh axis runs over, the one named last changes fastest.
Arguments:
- query_embed: bfloat16 [8, 16, 1024], P('group'), may hold values from -6 to 6
- teacher_scores: float32 [8, 16, 16, 32], P('group', 'pair'), may hold values from -9 to 9
- pair_owner: int32 [8, 16, 16, 32, 1], P('group', 'pair'), may hold values from 0 to 127; in each aligned block of 512 rows (0 to 511, 512 to 1023, ..., all dimensions but the last counted through in order) at most 8 rows name the same one
- pair_row: int32 [8, 16, 16, 32], P('group', 'pair'), may hold values from 0 to 2047
- passage_hidden: bfloat16 [262144, 1024], P(('group', 'pair')), may hold values from -24 to 24
- projection: bfloat16 [1024, 1024], replicated, may hold values from -0.1875 to 0.1875
Outputs:
- query_loss: float32 [8, 16], P('group', 'pair')
- query_grad: float32 [8, 16, 1024], P('group', 'pair')
- hidden_grad: bfloat16 [262144, 1024], P(('group', 'pair'))
- projection_grad: float32 [1024, 1024], P(('group', 'pair'))
The draws below stay inside these ranges and needn't reach their ends.
Inputs may be any that keep to these rules, and one draw needn't show every extreme that they name: `pair_owner`: owners are numbered with group as the slower index. Among the 512 candidates held by one device, at most 8 name the same owner, and every draw has a device and an owner with exactly 8. `pair_row`: A passage may be named by several candidates.
All inputs are finite; a program needn't handle non-finite values.
Results may differ from the reference program's by a relative error of at most 0.022.
Values may be sent and summed in bfloat16 or wider, within the bound.
A program may use at most 128 MiB of HBM per device.

```python
import math
import jax
import jax.numpy as jnp
import numpy as np
from jax import lax

D = 1024
K = 512
PASS_DEV = 2048
Q_GRP = 16
K_DEV = 32
PASSAGES = 262144
CAP = 8
N_GROUP = 8
N_PAIR = 16
DEVICES = 128


def plant(entries, key, smallest, high):
    index_at = [jax.random.randint(jax.random.fold_in(key, axis), (), 0, length) for axis, length in enumerate(entries.shape)]
    main_axis = entries.shape.index(max(entries.shape))
    neighbour = index_at[:main_axis] + [(index_at[main_axis] + 1) % entries.shape[main_axis]] + index_at[main_axis + 1:]
    return entries.at[tuple(index_at)].set(smallest).at[tuple(neighbour)].set(high)


def strengthened(values, key, source, target, blocks, factor):
    def block_of(position):
        return (jnp.arange(values.shape[position]) // (values.shape[position] // blocks)).reshape((-1,) + (1,) * (values.ndim - 1 - position))

    first = jax.random.permutation(key, blocks)[block_of(target)]
    second = (block_of(target) + blocks // 2) % blocks
    return jnp.where((block_of(source) == first) | (block_of(source) == second), factor * values, values)


def level_of(own_key, shape, cuts, least, high):
    loudness = 1.0
    for position, blocks in cuts:
        draws = jax.random.uniform(jax.random.fold_in(jax.random.fold_in(own_key, 6), position), (blocks,), jnp.float32, least / len(cuts), high / len(cuts))
        loudness = loudness * jnp.repeat(jnp.exp(draws), shape[position] // blocks).reshape((-1,) + (1,) * (len(shape) - 1 - position))
    return loudness


def deal_out(rng, own, number, rows, count, top, bound, slope):
    ranking = jax.random.permutation(rng, count)
    heavy_load, usual = shares(count, rows * top, bound, slope, True), shares(count, rows * top, bound, slope, False)
    places = jnp.arange(count)

    def named(tallies, offset_by):
        used = int((tallies > 0).sum())
        fixed = max(1, used // 4)
        moved = fixed + (places - fixed + offset_by * (used - fixed)) % max(1, count - fixed)
        return jnp.zeros((count,), jnp.int32).at[ranking[jnp.where(places < fixed, places, moved)]].set(jnp.asarray(tallies, jnp.int32))

    tallies = jnp.where(number % 4 == 0, named(heavy_load, number // 4), named(usual, number - number // 4 - 1))
    mixed = jax.random.permutation(jax.random.fold_in(own, 3), count)
    giver, receiver = mixed[0:count // 2 * 2:2], mixed[1:count // 2 * 2:2]
    room = jnp.minimum(tallies[giver] - 1, bound - tallies[receiver]) // 2
    room = jnp.where((giver == ranking[0]) | (receiver == ranking[0]) | (tallies[receiver] == 0), 0, jnp.maximum(room, 0))
    moved = jax.random.randint(jax.random.fold_in(own, 4), (count // 2,), 0, 1 << 20) % (room + 1)
    tallies = tallies.at[giver].add(-moved).at[receiver].add(moved)
    items = jnp.searchsorted(jnp.cumsum(tallies), jnp.arange(rows * top), side="right").astype(jnp.int32)
    table = items.reshape(top, rows).T
    table = table[jax.random.permutation(jax.random.fold_in(own, 1), rows)]
    offset_by = jax.random.randint(jax.random.fold_in(own, 2), (rows, 1), 0, top)
    return jnp.take_along_axis(table, (jnp.arange(top)[None, :] + offset_by) % top, axis=1)


def shares(number_of, total, limit, lean, full):
    loads = [(1 << 20) // math.isqrt(rank ** lean) + 1 for rank in range(1, number_of + 1)]
    largest = limit if full else min(limit, max(-(-total // number_of), total * loads[0] // sum(loads)))
    least = 1 if total - largest >= number_of - 1 else 0
    counts, surplus = [largest] + [least] * (number_of - 1), total - largest - least * (number_of - 1)
    while surplus > 0:
        movable = [i for i in range(1, number_of) if counts[i] < largest] or [i for i in range(1, number_of) if counts[i] < limit]
        mass, budget = sum([loads[i] for i in movable]), surplus
        for i in movable:
            more = min(limit - counts[i], max(1, budget * loads[i] // mass), surplus)
            counts[i] = counts[i] + more
            surplus = surplus - more
    return np.array(counts)


def normal_values(own_key, dims, deviation, bound, shards=(), kind=jnp.bfloat16):
    drawn = deviation * jax.random.normal(own_key, dims, jnp.float32)
    if shards:
        drawn = drawn * level_of(own_key, dims, shards, -0.22, 0.18)
    return jnp.clip(drawn, -bound, bound).astype(kind)


def bell_draw_with(key, extent, spread, reach, shards, heavy, held_as=jnp.bfloat16):
    values = spread * jax.random.normal(key, extent, jnp.float32)
    if shards:
        values = values * level_of(key, extent, shards, -0.22, 0.18)
    return jnp.clip(strengthened(values, jax.random.fold_in(key, 3), *heavy), -reach, reach).astype(held_as)


def setup_inputs(seed: int = 0) -> dict:
    key_list = jax.random.split(jax.random.key(seed), 7)
    query_embed = normal_values(key_list[0], (N_GROUP, Q_GRP, D), 1.0, 6.0, ((0, 8),))
    teacher_scores = normal_values(key_list[1], (N_GROUP, N_PAIR, Q_GRP, K_DEV), 1.5, 9.0, ((0, 8), (1, 16)), jnp.float32)
    pair_owner_keys = jax.random.split(jax.random.fold_in(key_list[2], 1), N_GROUP * N_PAIR * Q_GRP * K_DEV // (Q_GRP * K_DEV))
    pair_owner_turns = jax.random.permutation(jax.random.fold_in(key_list[2], 3), N_GROUP * N_PAIR * Q_GRP * K_DEV // (Q_GRP * K_DEV))
    pair_owner = jax.vmap(lambda own, number: deal_out(jax.random.fold_in(key_list[2], 2), own, number, Q_GRP * K_DEV, DEVICES, 1, CAP, 2))(pair_owner_keys, pair_owner_turns).reshape((N_GROUP, N_PAIR, Q_GRP, K_DEV, 1))
    pair_row = plant(jax.random.randint(key_list[3], (N_GROUP, N_PAIR, Q_GRP, K_DEV), 0, PASS_DEV), jax.random.fold_in(key_list[3], 1), 0, PASS_DEV - 1).astype(jnp.int32)
    passage_hidden = bell_draw_with(key_list[4], (PASSAGES, D), 1.0, 24.0, ((0, 128),), (0, 1, 128, 5.5))
    projection = normal_values(key_list[5], (D, D), D ** -0.5, 0.1875)
    return {"query_embed": query_embed, "teacher_scores": teacher_scores, "pair_owner": pair_owner, "pair_row": pair_row, "passage_hidden": passage_hidden, "projection": projection}


loss_scale = 1024.0

def reference(query_embed, teacher_scores, pair_owner, pair_row, passage_hidden, projection):
    inv_root = 1.0 / math.sqrt(D)
    spearman_den = float(K * (K * K - 1))
    embedded = jnp.dot(passage_hidden, projection, preferred_element_type=jnp.float32).astype(jnp.bfloat16)
    passage = (pair_owner[..., 0] * PASS_DEV + pair_row).astype(jnp.int32)
    passage = jnp.transpose(passage, (0, 2, 1, 3)).reshape(N_GROUP, Q_GRP, K).astype(jnp.int32)
    teacher_all = jnp.transpose(teacher_scores, (0, 2, 1, 3)).reshape(N_GROUP, Q_GRP, K)

    def per_group(group_args):
        queries, passage_ids, teacher_row = group_args
        vectors = jnp.take(embedded, passage_ids, axis=0).astype(jnp.float32)
        queries_f = queries.astype(jnp.float32)
        scores = jnp.einsum('qd,qkd->qk', queries_f, vectors, precision=lax.Precision.HIGHEST) * inv_root
        soft_step = jax.nn.sigmoid((scores[:, None, :] - scores[:, :, None]) * 2.0)
        rank_student = 0.5 + lax.optimization_barrier(jnp.sum(soft_step, -1))
        rank_teacher = 0.5 + lax.optimization_barrier(jnp.sum(jax.nn.sigmoid((teacher_row[:, None, :] - teacher_row[:, :, None]) * 2.0), -1))
        rank_gap = rank_student - rank_teacher
        query_loss = 6.0 * lax.optimization_barrier(jnp.sum(rank_gap * rank_gap, axis=1)) / spearman_den
        rank_grad = loss_scale * 12.0 * rank_gap / spearman_den
        slopes = soft_step * (1.0 - soft_step)
        score_grad = 2.0 * (lax.optimization_barrier(jnp.sum(slopes * rank_grad[:, None, :], -1)) - rank_grad * lax.optimization_barrier(jnp.sum(slopes, -1)))
        pair_grad = (score_grad[:, :, None] * queries_f[:, None, :] * inv_root).astype(jnp.bfloat16)
        query_grad = lax.optimization_barrier(jnp.sum(score_grad[:, :, None] * vectors, axis=1)) * inv_root
        return (query_loss, query_grad, pair_grad)
    query_loss, query_grad, pair_grad = lax.map(per_group, (query_embed, passage, teacher_all))
    embed_grad = jnp.zeros((PASSAGES, D), jnp.float32).at[passage.reshape(-1)].add(pair_grad.reshape(-1, D).astype(jnp.float32))
    grad_rounded = embed_grad.astype(jnp.bfloat16)
    hidden_grad = jnp.dot(grad_rounded, projection.T, preferred_element_type=jnp.float32).astype(jnp.bfloat16)
    projection_grad = jnp.dot(passage_hidden.T, grad_rounded, preferred_element_type=jnp.float32)
    return (query_loss, query_grad, hidden_grad, projection_grad)
```

```python
import math

import jax
import jax.numpy as jnp
from jax import lax
from jax.sharding import PartitionSpec as P

loss_scale = 1024.0
f32, bf16, i32 = jnp.float32, jnp.bfloat16, jnp.int32


def iota(shape, dim):
    return lax.broadcasted_iota(i32, shape, dim)


def dot(a, b, ca, cb):
    return lax.dot_general(a, b, (((ca,), (cb,)), ((), ())), preferred_element_type=f32)


def halves(x):
    high = x.astype(bf16)
    return high, (x - high.astype(f32)).astype(bf16)


def shards(query_embed, teacher_scores, pair_owner, pair_row, passage_hidden, projection):
    width = query_embed.shape[2]
    q_rows = query_embed.shape[1]
    cand = teacher_scores.shape[3]
    n_pair, n_group = lax.axis_size("pair"), lax.axis_size("group")
    n_dev = n_pair * n_group
    cap = max(2, 2 * q_rows * cand // n_dev)
    slots = n_pair * cap
    k_all = cand * n_pair
    queries_n = n_group * q_rows
    rows = passage_hidden.shape[0]
    den = float(k_all * (k_all * k_all - 1))
    inv_root = 1.0 / math.sqrt(width)
    r = lax.axis_index("pair")
    owner = pair_owner.reshape(1, q_rows * cand)
    row = pair_row.reshape(1, q_rows * cand)
    n_own = q_rows * cand
    lane = iota((1, n_own), 1)
    owner_hot = iota((n_dev, n_own), 0) == owner
    owner_b = owner_hot.astype(bf16)
    before = (iota((n_own, n_own), 0) < iota((n_own, n_own), 1)).astype(bf16)
    seen = dot(owner_b, before, 1, 0)
    slot = jnp.sum(jnp.where(owner_hot, seen, 0.0), axis=0, keepdims=True).astype(i32)
    at_slot = iota((slots, n_own), 0) == slot + r * cap
    high = (row >> 4) + 1
    low = (row & 15) * 16 + lane // cand
    req = dot(owner_b, jnp.where(at_slot, high, 0).astype(bf16), 1, 1) * 256.0 + dot(
        owner_b, jnp.where(at_slot, low, 0).astype(bf16), 1, 1
    )
    q_all = lax.all_gather(query_embed[0], "group", axis=0, tiled=True)
    got = lax.all_to_all(req, ("group", "pair"), split_axis=0, concat_axis=0, tiled=True)
    packed = got.reshape(n_group, n_pair, slots).sum(1).reshape(1, n_group * slots).astype(i32)
    pq = dot(q_all, projection, 1, 1).astype(bf16)
    s_t = dot(pq, passage_hidden, 1, 1) * inv_root
    s_hi, s_lo = halves(s_t)
    place = (iota((rows, n_group * slots), 0) == (packed >> 4) - 16).astype(bf16)
    z = dot(s_hi, place, 1, 0) + dot(s_lo, place, 1, 0)
    slot_query = (packed & 15) + q_rows * (iota((1, n_group * slots), 1) // slots)
    slot_score = jnp.sum(
        jnp.where(iota((queries_n, n_group * slots), 0) == slot_query, z, 0.0), axis=0
    ).reshape(n_group, 1, slots)
    to_send = jnp.broadcast_to(slot_score, (n_group, n_pair, slots)).reshape(n_dev, slots)
    table = lax.all_to_all(to_send, ("group", "pair"), split_axis=0, concat_axis=0, tiled=True)
    tags = (owner * cap + slot).reshape(q_rows, cand)
    tags_k = lax.all_to_all(tags, "pair", split_axis=0, concat_axis=0, tiled=True).reshape(1, k_all)
    teach_k = lax.all_to_all(
        teacher_scores.reshape(q_rows, cand), "pair", split_axis=0, concat_axis=0, tiled=True
    ).reshape(1, k_all)
    k_owner = (iota((n_dev, k_all), 0) == tags_k // cap).astype(bf16)
    k_slot = (iota((slots, k_all), 0) == tags_k % cap + cap * (iota((1, k_all), 1) // cand)).astype(f32)
    t_hi, t_lo = halves(table.T)
    picked = dot(t_hi, k_owner, 1, 0) + dot(t_lo, k_owner, 1, 0)
    s_k = jnp.sum(picked * k_slot, axis=0, keepdims=True)
    tanh_s = jnp.tanh(s_k.T - s_k)
    tanh_t = jnp.tanh(teach_k.T - teach_k)
    gap = 0.5 * (jnp.sum(tanh_s, 0, keepdims=True) - jnp.sum(tanh_t, 0, keepdims=True))
    loss = 6.0 * jnp.sum(gap * gap, axis=1, keepdims=True) / den
    grad = loss_scale * 12.0 * gap / den
    s_grad = 0.5 * jnp.sum((grad.T - grad) * (1.0 - tanh_s * tanh_s), axis=0, keepdims=True)
    values = dot(k_owner, (k_slot * s_grad).astype(bf16), 1, 1)
    back = lax.all_to_all(values, ("group", "pair"), split_axis=0, concat_axis=0, tiled=True)
    same_group = iota((queries_n, n_group * slots), 0) // q_rows == iota((queries_n, n_group * slots), 1) // slots
    spread = jnp.where(same_group, jnp.tile(back, (1, n_group)), 0.0).astype(bf16)
    w_t = dot(place, spread, 1, 1).astype(bf16)
    hidden_grad = (dot(w_t, pq, 1, 0) * inv_root).astype(bf16)
    u_part = dot(w_t, passage_hidden, 0, 0).astype(bf16)
    u_rows = lax.all_to_all(u_part, ("group", "pair"), split_axis=0, concat_axis=0, tiled=True)
    u_cols = lax.all_to_all(u_part.T, ("group", "pair"), split_axis=0, concat_axis=0, tiled=True)
    u_row = jnp.sum(u_rows.astype(f32), 0, keepdims=True) * inv_root
    u_col = jnp.sum(u_cols.astype(f32).reshape(n_dev, width // n_dev, queries_n), 0) * inv_root
    r_hi, r_lo = halves(u_row)
    c_hi, c_lo = halves(u_col)
    query_grad = dot(r_hi, projection, 1, 0) + dot(r_lo, projection, 1, 0)
    projection_grad = dot(c_hi, q_all, 1, 0) + dot(c_lo, q_all, 1, 0)
    return loss, query_grad.reshape(1, 1, width), hidden_grad, projection_grad


def solution(mesh):
    placed = (
        P("group", None, None),
        P("group", "pair", None, None),
        P("group", "pair", None, None, None),
        P("group", "pair", None, None),
        P(("group", "pair"), None),
        P(),
    )
    return jax.shard_map(
        shards,
        mesh=mesh,
        in_specs=placed,
        out_specs=(
            P("group", "pair"),
            P("group", "pair", None),
            P(("group", "pair"), None),
            P(("group", "pair"), None),
        ),
        check_vma=False,
    )
```

```python
import functools
import math

import jax
import jax.numpy as jnp
from jax import lax
from jax.experimental import pallas as pl
from jax.experimental.pallas import tpu as pltpu
from jax.sharding import PartitionSpec as P

MESH = pl.DeviceIdType.MESH
loss_scale = 1024.0
f32, bf16, i32 = jnp.float32, jnp.bfloat16, jnp.int32


def iota(shape, dim):
    return lax.broadcasted_iota(i32, shape, dim)


def dot(a, b, ca, cb):
    return lax.dot_general(a, b, (((ca,), (cb,)), ((), ())), preferred_element_type=f32)


def halves(x):
    high = x.astype(bf16)
    return high, (x - high.astype(f32)).astype(bf16)


def flat_row(x):
    return jnp.concatenate([x[i : i + 1, :] for i in range(x.shape[0])], axis=1)


def step_kernel(
    n_group, n_pair, cap,
    q_ref, teach_ref, owner_ref, row_ref, hid_hbm, proj_hbm,
    wt_ref, pq_ref, loss_ref, qg_ref, pg_ref,
    hid, proj, q_all, req_out, req_in, key_out, key_in, score_out, score_in,
    value_out, value_in, place, tanh_s, u_wide, u_out, u_in,
    load_sem, send_sem, recv_sem,
):
    n_dev = n_group * n_pair
    q_rows, width = q_ref.shape
    cand = teach_ref.shape[1]
    n_own = q_rows * cand
    k_all = cand * n_pair
    slots = n_pair * cap
    rows = hid.shape[0]
    den = float(k_all * (k_all * k_all - 1))
    inv_root = 1.0 / math.sqrt(width)
    g, r = lax.axis_index("group"), lax.axis_index("pair")
    me = g * n_pair + r

    load_hid = pltpu.make_async_copy(hid_hbm, hid, load_sem.at[0])
    load_proj = pltpu.make_async_copy(proj_hbm, proj, load_sem.at[1])
    load_proj.start()
    load_hid.start()

    def peer(i):
        p = lax.rem(me + i, n_dev)
        return p, {"group": p // n_pair, "pair": lax.rem(p, n_pair)}

    barrier = pltpu.get_barrier_semaphore()

    def greet(i, carry):
        _, where = peer(i)
        pl.semaphore_signal(barrier, inc=1, device_id=where, device_id_type=MESH)
        return carry

    lax.fori_loop(1, n_dev, greet, 0)

    def send_all(number, source_of, source_me, target):
        def one(i, carry):
            p, where = peer(i)
            pltpu.make_async_remote_copy(
                src_ref=source_of(p),
                dst_ref=target.at[me],
                send_sem=send_sem.at[number],
                recv_sem=recv_sem.at[number],
                device_id=where,
                device_id_type=MESH,
            ).start()
            return carry

        lax.fori_loop(1, n_dev, one, 0)
        pltpu.make_async_copy(source_me, target.at[me], recv_sem.at[number]).start()

    def all_here(number, target):
        pltpu.make_async_copy(target, target, recv_sem.at[number]).wait()

    def all_sent(number, target, count):
        part = target.at[pl.ds(0, count)]
        pltpu.make_async_copy(part, part, send_sem.at[number]).wait()

    own, row = flat_row(owner_ref[...]), flat_row(row_ref[...])
    lane = iota((1, n_own), 1)
    hot = iota((n_dev, n_own), 0) == own
    hot_f = jnp.where(hot, 1.0, 0.0)
    hot_b = hot_f.astype(bf16)
    before = jnp.where(iota((n_own, n_own), 0) < iota((n_own, n_own), 1), 1.0, 0.0).astype(bf16)
    seen = dot(hot_b, before, 1, 0)
    slot = jnp.sum(hot_f * seen, axis=0, keepdims=True).astype(i32)
    at_slot = iota((slots, n_own), 0) == slot + r * cap
    high = ((row >> 4) + 1).astype(f32)
    low = ((row & 15) * 16 + lane // cand).astype(f32)
    req = dot(hot_b, jnp.where(at_slot, high, 0.0).astype(bf16), 1, 1) * 256.0 + dot(
        hot_b, jnp.where(at_slot, low, 0.0).astype(bf16), 1, 1
    )
    req_out[:, 0, :] = req
    tag = (own * cap + slot).astype(f32)
    for q in range(q_rows):
        key_out[q, :, 0:cand] = tag[:, q * cand : (q + 1) * cand]
        key_out[q, :, cand : 2 * cand] = teach_ref[q : q + 1, :]

    pl.semaphore_wait(barrier, n_dev - 1)

    def send_q(i, carry):
        other = lax.rem(g + i, n_group)
        pltpu.make_async_remote_copy(
            src_ref=q_ref,
            dst_ref=q_all.at[g],
            send_sem=send_sem.at[0],
            recv_sem=recv_sem.at[0],
            device_id={"group": other, "pair": r},
            device_id_type=MESH,
        ).start()
        return carry

    lax.fori_loop(1, n_group, send_q, 0)
    pltpu.make_async_copy(q_ref, q_all.at[g], recv_sem.at[0]).start()
    send_all(1, lambda p: req_out.at[p], req_out.at[me], req_in)

    def send_key(i, carry):
        other = lax.rem(r + i, n_pair)
        pltpu.make_async_remote_copy(
            src_ref=key_out.at[other],
            dst_ref=key_in.at[r],
            send_sem=send_sem.at[2],
            recv_sem=recv_sem.at[2],
            device_id={"group": g, "pair": other},
            device_id_type=MESH,
        ).start()
        return carry

    lax.fori_loop(1, n_pair, send_key, 0)
    pltpu.make_async_copy(key_out.at[r], key_in.at[r], recv_sem.at[2]).start()

    all_here(0, q_all)
    load_proj.wait()
    queries_n = n_group * q_rows
    q_flat = q_all[...].reshape(queries_n, width)
    pq = dot(q_flat, proj[...], 1, 1).astype(bf16)
    pq_ref[...] = pq
    load_hid.wait()
    s_t = (dot(hid[...], pq, 1, 1) * inv_root).T
    s_hi, s_lo = halves(s_t)

    all_here(1, req_in)
    packed = jnp.sum(req_in[...].reshape(n_group, n_pair, 1, slots), axis=1).astype(i32)
    span = 2
    for h in range(n_group // span):
        rows_of = [packed[h * span + i] for i in range(span)]
        here = jnp.concatenate(rows_of, axis=1)
        mark = jnp.where(iota((rows, span * slots), 0) == (here >> 4) - 16, 1.0, 0.0).astype(bf16)
        place[:, h * span * slots : (h + 1) * span * slots] = mark
        lo_q, hi_q = h * span * q_rows, (h + 1) * span * q_rows
        z = dot(jnp.concatenate([s_hi[lo_q:hi_q], s_lo[lo_q:hi_q]], axis=0), mark, 1, 0)
        z = z[: span * q_rows] + z[span * q_rows :]
        of_query = (here & 15) + q_rows * (iota((1, span * slots), 1) // slots)
        value = jnp.sum(
            jnp.where(iota((span * q_rows, span * slots), 0) == of_query, z, 0.0), axis=0, keepdims=True
        )
        for i in range(span):
            score_out[h * span + i] = value[:, i * slots : (i + 1) * slots]
    send_all(3, lambda p: score_out.at[p // n_pair], score_out.at[g], score_in)

    all_here(2, key_in)
    keys = key_in[:, 0, :]
    tags = flat_row(keys[:, 0:cand]).astype(i32)
    teach = flat_row(keys[:, cand : 2 * cand])
    k_owner = jnp.where(iota((n_dev, k_all), 0) == tags // cap, 1.0, 0.0).astype(bf16)
    k_slot = jnp.where(
        iota((slots, k_all), 0) == tags % cap + cap * (iota((1, k_all), 1) // cand), 1.0, 0.0
    )

    def column(x):
        return jnp.broadcast_to(x, (128, k_all)).T

    blocks = [(j * 128, (j + 1) * 128) for j in range(k_all // 128)]
    t_col = column(teach)
    t_sum = jnp.concatenate(
        [jnp.sum(jnp.tanh(t_col - teach[:, a:b]), axis=0, keepdims=True) for a, b in blocks], axis=1
    )
    all_here(3, score_in)
    t_hi, t_lo = halves(score_in[:, 0, :].T)
    picked = dot(jnp.concatenate([t_hi, t_lo], axis=0), k_owner, 1, 0)
    s_k = jnp.sum((picked[:slots] + picked[slots:]) * k_slot, axis=0, keepdims=True)
    s_col = column(s_k)
    sums = []
    for a, b in blocks:
        soft = jnp.tanh(s_col - s_k[:, a:b])
        tanh_s[:, a:b] = soft
        sums.append(jnp.sum(soft, axis=0, keepdims=True))
    gap = 0.5 * (jnp.concatenate(sums, axis=1) - t_sum)
    loss_ref[...] = 6.0 * jnp.sum(gap * gap, axis=1, keepdims=True) / den
    grad = gap * (loss_scale * 12.0 / den)
    g_col = column(grad)
    parts = []
    for a, b in blocks:
        soft = tanh_s[:, a:b]
        parts.append(
            jnp.sum((g_col - grad[:, a:b]) * (1.0 - soft * soft), axis=0, keepdims=True)
        )
    s_grad = 0.5 * jnp.concatenate(parts, axis=1)
    value_out[:, 0, :] = dot(k_owner, (k_slot * s_grad).astype(bf16), 1, 1)
    send_all(4, lambda p: value_out.at[p], value_out.at[me], value_in)

    all_here(4, value_in)
    back = value_in[:, 0, :]
    spread = jnp.concatenate(
        [jnp.where(iota((n_dev, slots), 0) // n_pair == h, back, 0.0) for h in range(n_group)], axis=1
    ).astype(bf16)
    w_t = dot(place[...], spread, 1, 1).astype(bf16)
    wt_ref[...] = w_t
    u = dot(w_t, hid[...], 0, 0)
    per = width // n_dev
    for b in range(width // 128):
        u_wide[:, b, :] = u[:, b * 128 : (b + 1) * 128]
    u_wide[:, width // 128 :, :] = u.T.reshape(n_dev, per, 128)
    u_out[...] = u_wide[...].astype(bf16)
    send_all(5, lambda p: u_out.at[p], u_out.at[me], u_in)
    all_here(5, u_in)
    total = jnp.sum(u_in[...].astype(f32), axis=0) * inv_root
    n_b = width // 128
    u_row, u_col = total[:n_b], total[n_b:]
    wide = jnp.concatenate(
        [jnp.where(iota((n_b, 128), 0) == b, u_row, 0.0) for b in range(n_b)], axis=1
    )
    w_hi, w_lo = halves(wide)
    query_grad = dot(jnp.concatenate([w_hi, w_lo], axis=0), proj[...], 1, 0)
    qg_ref[...] = jnp.sum(query_grad, axis=0, keepdims=True)
    c_hi, c_lo = halves(u_col)
    proj_grad = dot(jnp.concatenate([c_hi, c_lo], axis=0), q_flat, 1, 0)
    pg_ref[...] = proj_grad[:per] + proj_grad[per:]

    part = q_all.at[pl.ds(0, n_group - 1)]
    pltpu.make_async_copy(part, part, send_sem.at[0]).wait()
    all_sent(1, req_in, n_dev - 1)
    all_sent(2, key_in, n_pair - 1)
    all_sent(3, score_in, n_dev - 1)
    all_sent(4, value_in, n_dev - 1)
    all_sent(5, u_in, n_dev - 1)


def finish_kernel(inv_root, wt_ref, pq_ref, loss_ref, qg_ref, pg_ref, hg_out, loss_out, qg_out, pg_out):
    hg_out[...] = (dot(wt_ref[...], pq_ref[...], 1, 0) * inv_root).astype(bf16)

    @pl.when(pl.program_id(0) == 0)
    def _():
        loss_out[...] = loss_ref[...]
        qg_out[...] = qg_ref[...]
        pg_out[...] = pg_ref[...]


def shards(query_embed, teacher_scores, pair_owner, pair_row, passage_hidden, projection):
    width = query_embed.shape[2]
    q_rows = query_embed.shape[1]
    cand = teacher_scores.shape[3]
    n_pair, n_group = lax.axis_size("pair"), lax.axis_size("group")
    n_dev = n_pair * n_group
    cap = max(2, 2 * q_rows * cand // n_dev)
    slots = n_pair * cap
    k_all = cand * n_pair
    queries_n = n_group * q_rows
    rows = passage_hidden.shape[0]
    per = width // n_dev
    vmem = pl.BlockSpec(memory_space=pltpu.VMEM)
    hbm = pl.BlockSpec(memory_space=pl.ANY)
    message = pltpu.VMEM((n_dev, 1, slots), f32)
    w_t, pq, loss, query_grad, projection_grad = pl.pallas_call(
        functools.partial(step_kernel, n_group, n_pair, cap),
        out_shape=(
            jax.ShapeDtypeStruct((rows, queries_n), bf16),
            jax.ShapeDtypeStruct((queries_n, width), bf16),
            jax.ShapeDtypeStruct((1, 1), f32),
            jax.ShapeDtypeStruct((1, width), f32),
            jax.ShapeDtypeStruct((per, width), f32),
        ),
        in_specs=[vmem, vmem, vmem, vmem, hbm, hbm],
        out_specs=(vmem,) * 5,
        scratch_shapes=[
            pltpu.VMEM((rows, width), bf16),
            pltpu.VMEM((width, width), bf16),
            pltpu.VMEM((n_group, q_rows, width), bf16),
            message,
            message,
            pltpu.VMEM((q_rows, 1, 128), f32),
            pltpu.VMEM((n_pair, 1, 128), f32),
            pltpu.VMEM((n_group, 1, slots), f32),
            message,
            message,
            message,
            pltpu.VMEM((rows, n_group * slots), bf16),
            pltpu.VMEM((k_all, k_all), f32),
            pltpu.VMEM((n_dev, 16, 128), f32),
            pltpu.VMEM((n_dev, 16, 128), bf16),
            pltpu.VMEM((n_dev, 16, 128), bf16),
            pltpu.SemaphoreType.DMA((2,)),
            pltpu.SemaphoreType.DMA((6,)),
            pltpu.SemaphoreType.DMA((6,)),
        ],
        compiler_params=pltpu.CompilerParams(collective_id=0, has_side_effects=True),
        name="step",
    )(
        query_embed[0],
        teacher_scores.reshape(q_rows, cand),
        pair_owner.reshape(q_rows, cand),
        pair_row.reshape(q_rows, cand),
        passage_hidden,
        projection,
    )
    tile = 512

    def whole(shape):
        return pl.BlockSpec(shape, lambda i: (0, 0))

    hidden_grad, loss, query_grad, projection_grad = pl.pallas_call(
        functools.partial(finish_kernel, 1.0 / math.sqrt(width)),
        grid=(rows // tile,),
        out_shape=(
            jax.ShapeDtypeStruct((rows, width), bf16),
            jax.ShapeDtypeStruct((1, 1), f32),
            jax.ShapeDtypeStruct((1, width), f32),
            jax.ShapeDtypeStruct((per, width), f32),
        ),
        in_specs=[
            pl.BlockSpec((tile, queries_n), lambda i: (i, 0)),
            whole((queries_n, width)),
            whole((1, 1)),
            whole((1, width)),
            whole((per, width)),
        ],
        out_specs=(
            pl.BlockSpec((tile, width), lambda i: (i, 0)),
            whole((1, 1)),
            whole((1, width)),
            whole((per, width)),
        ),
        name="finish",
    )(w_t, pq, loss, query_grad, projection_grad)
    return loss, query_grad.reshape(1, 1, width), hidden_grad, projection_grad


def solution(mesh):
    placed = (
        P("group", None, None),
        P("group", "pair", None, None),
        P("group", "pair", None, None, None),
        P("group", "pair", None, None),
        P(("group", "pair"), None),
        P(),
    )
    return jax.shard_map(
        shards,
        mesh=mesh,
        in_specs=placed,
        out_specs=(
            P("group", "pair"),
            P("group", "pair", None),
            P(("group", "pair"), None),
            P(("group", "pair"), None),
        ),
        check_vma=False,
    )
```

```python
import functools
import math

import jax
import jax.numpy as jnp
from jax import lax
from jax.experimental import pallas as pl
from jax.experimental.pallas import tpu as pltpu
from jax.sharding import PartitionSpec as P

MESH = pl.DeviceIdType.MESH
loss_scale = 1024.0
f32, bf16, i32 = jnp.float32, jnp.bfloat16, jnp.int32


def iota(shape, dim):
    return lax.broadcasted_iota(i32, shape, dim)


def dot(a, b, ca, cb):
    return lax.dot_general(a, b, (((ca,), (cb,)), ((), ())), preferred_element_type=f32)


def halves(x):
    high = x.astype(bf16)
    return high, (x - high.astype(f32)).astype(bf16)


def flat_row(x):
    return jnp.concatenate([x[i : i + 1, :] for i in range(x.shape[0])], axis=1)


def step_kernel(
    n_group, n_pair, cap,
    q_hbm, teach_hbm, owner_hbm, row_hbm, hid_hbm, proj_hbm,
    hg_ref, loss_ref, qg_ref, pg_ref,
    q_ref, teach_ref, owner_ref, row_ref,
    hid, proj, q_all, req_out, req_in, key_out, key_in, score_out, score_in,
    value_out, value_in, place, tanh_s, u_wide, u_out, u_in,
    load_sem, send_sem, recv_sem,
):
    n_dev = n_group * n_pair
    q_rows, width = q_ref.shape
    cand = teach_ref.shape[1]
    n_own = q_rows * cand
    k_all = cand * n_pair
    slots = n_pair * cap
    rows = hid.shape[0]
    den = float(k_all * (k_all * k_all - 1))
    inv_root = 1.0 / math.sqrt(width)
    g, r = lax.axis_index("group"), lax.axis_index("pair")
    me = g * n_pair + r

    loads = [
        pltpu.make_async_copy(source, target, load_sem.at[n])
        for n, (source, target) in enumerate(
            [(owner_hbm, owner_ref), (row_hbm, row_ref), (teach_hbm, teach_ref), (q_hbm, q_ref),
             (proj_hbm, proj), (hid_hbm, hid)]
        )
    ]
    for load in loads:
        load.start()

    def others(visit):
        def ring(i, carry):
            group = lax.rem(g + i, n_group)
            for pair in range(n_pair):
                visit(group, pair)
            return carry

        def row_of_pairs(i, carry):
            visit(g, lax.rem(r + i, n_pair))
            return carry

        lax.fori_loop(1, n_group, ring, 0)
        lax.fori_loop(1, n_pair, row_of_pairs, 0, unroll=True)

    barrier = pltpu.get_barrier_semaphore()

    def greet(group, pair):
        pl.semaphore_signal(
            barrier, inc=1, device_id={"group": group, "pair": pair}, device_id_type=MESH
        )

    others(greet)

    def send_all(number, source_of, target):
        def one(group, pair):
            pltpu.make_async_remote_copy(
                src_ref=source_of(group, pair),
                dst_ref=target.at[me],
                send_sem=send_sem.at[number],
                recv_sem=recv_sem.at[number],
                device_id={"group": group, "pair": pair},
                device_id_type=MESH,
            ).start()

        pltpu.make_async_copy(source_of(g, r), target.at[me], recv_sem.at[number]).start()
        others(one)

    def all_here(number, target):
        pltpu.make_async_copy(target, target, recv_sem.at[number]).wait()

    def all_sent(number, target, count):
        part = target.at[pl.ds(0, count)]
        pltpu.make_async_copy(part, part, send_sem.at[number]).wait()

    for load in loads[:3]:
        load.wait()
    own, row = flat_row(owner_ref[...]), flat_row(row_ref[...])
    lane = iota((1, n_own), 1)
    hot = iota((n_dev, n_own), 0) == own
    hot_f = jnp.where(hot, 1.0, 0.0)
    hot_b = hot_f.astype(bf16)
    before = jnp.where(iota((n_own, n_own), 0) < iota((n_own, n_own), 1), 1.0, 0.0).astype(bf16)
    seen = dot(hot_b, before, 1, 0)
    slot = jnp.sum(hot_f * seen, axis=0, keepdims=True).astype(i32)
    at_slot = iota((slots, n_own), 0) == slot + r * cap
    high = ((row >> 4) + 1).astype(f32)
    low = ((row & 15) * 16 + lane // cand).astype(f32)
    req = dot(hot_b, jnp.where(at_slot, high, 0.0).astype(bf16), 1, 1) * 256.0 + dot(
        hot_b, jnp.where(at_slot, low, 0.0).astype(bf16), 1, 1
    )
    req_out[:, 0, :] = req
    tag = (own * cap + slot).astype(f32)
    for q in range(q_rows):
        key_out[q, :, 0:cand] = tag[:, q * cand : (q + 1) * cand]
        key_out[q, :, cand : 2 * cand] = teach_ref[q : q + 1, :]

    loads[3].wait()
    pl.semaphore_wait(barrier, n_dev - 1)

    def send_q(i, carry):
        other = lax.rem(g + i, n_group)
        pltpu.make_async_remote_copy(
            src_ref=q_ref,
            dst_ref=q_all.at[g],
            send_sem=send_sem.at[0],
            recv_sem=recv_sem.at[0],
            device_id={"group": other, "pair": r},
            device_id_type=MESH,
        ).start()
        return carry

    lax.fori_loop(1, n_group, send_q, 0, unroll=True)
    pltpu.make_async_copy(q_ref, q_all.at[g], recv_sem.at[0]).start()
    send_all(1, lambda group, pair: req_out.at[group * n_pair + pair], req_in)

    def send_key(i, carry):
        other = lax.rem(r + i, n_pair)
        pltpu.make_async_remote_copy(
            src_ref=key_out.at[other],
            dst_ref=key_in.at[r],
            send_sem=send_sem.at[2],
            recv_sem=recv_sem.at[2],
            device_id={"group": g, "pair": other},
            device_id_type=MESH,
        ).start()
        return carry

    lax.fori_loop(1, n_pair, send_key, 0, unroll=True)
    pltpu.make_async_copy(key_out.at[r], key_in.at[r], recv_sem.at[2]).start()

    all_here(0, q_all)
    loads[4].wait()
    queries_n = n_group * q_rows
    q_flat = q_all[...].reshape(queries_n, width)
    pq = (dot(q_flat, proj[...], 1, 1) * inv_root).astype(bf16)
    loads[5].wait()
    s_t = dot(hid[...], pq, 1, 1).T
    s_hi, s_lo = halves(s_t)

    all_here(1, req_in)
    packed = jnp.sum(req_in[...].reshape(n_group, n_pair, 1, slots), axis=1).astype(i32)
    span = 2
    for h in range(n_group // span):
        rows_of = [packed[h * span + i] for i in range(span)]
        here = jnp.concatenate(rows_of, axis=1)
        mark = jnp.where(iota((rows, span * slots), 0) == (here >> 4) - 16, 1.0, 0.0).astype(bf16)
        place[:, h * span * slots : (h + 1) * span * slots] = mark
        lo_q, hi_q = h * span * q_rows, (h + 1) * span * q_rows
        z = dot(jnp.concatenate([s_hi[lo_q:hi_q], s_lo[lo_q:hi_q]], axis=0), mark, 1, 0)
        z = z[: span * q_rows] + z[span * q_rows :]
        of_query = (here & 15) + q_rows * (iota((1, span * slots), 1) // slots)
        value = jnp.sum(
            jnp.where(iota((span * q_rows, span * slots), 0) == of_query, z, 0.0), axis=0, keepdims=True
        )
        for i in range(span):
            score_out[h * span + i] = value[:, i * slots : (i + 1) * slots]
    send_all(3, lambda group, pair: score_out.at[group], score_in)

    all_here(2, key_in)
    keys = key_in[:, 0, :]
    tags = flat_row(keys[:, 0:cand]).astype(i32)
    teach = flat_row(keys[:, cand : 2 * cand])
    k_owner = jnp.where(iota((n_dev, k_all), 0) == tags // cap, 1.0, 0.0).astype(bf16)
    k_slot = jnp.where(
        iota((slots, k_all), 0) == tags % cap + cap * (iota((1, k_all), 1) // cand), 1.0, 0.0
    )

    def column(x):
        return jnp.broadcast_to(x, (128, k_all)).T

    blocks = [(j * 128, (j + 1) * 128) for j in range(k_all // 128)]
    t_col = column(teach)
    t_sum = jnp.concatenate(
        [jnp.sum(jnp.tanh(t_col - teach[:, a:b]), axis=0, keepdims=True) for a, b in blocks], axis=1
    )
    all_here(3, score_in)
    t_hi, t_lo = halves(score_in[:, 0, :].T)
    picked = dot(jnp.concatenate([t_hi, t_lo], axis=0), k_owner, 1, 0)
    s_k = jnp.sum((picked[:slots] + picked[slots:]) * k_slot, axis=0, keepdims=True)
    s_col = column(s_k)
    sums = []
    for a, b in blocks:
        soft = jnp.tanh(s_col - s_k[:, a:b])
        tanh_s[:, a:b] = soft
        sums.append(jnp.sum(soft, axis=0, keepdims=True))
    gap = 0.5 * (jnp.concatenate(sums, axis=1) - t_sum)
    loss_ref[...] = jnp.broadcast_to(6.0 * jnp.sum(gap * gap, axis=1, keepdims=True) / den, (1, 128))
    grad = gap * (loss_scale * 12.0 / den)
    g_col = column(grad)
    parts = []
    for a, b in blocks:
        soft = tanh_s[:, a:b]
        parts.append(
            jnp.sum((g_col - grad[:, a:b]) * (1.0 - soft * soft), axis=0, keepdims=True)
        )
    s_grad = 0.5 * jnp.concatenate(parts, axis=1)
    value_out[:, 0, :] = dot(k_owner, (k_slot * s_grad).astype(bf16), 1, 1)
    send_all(4, lambda group, pair: value_out.at[group * n_pair + pair], value_in)

    all_here(4, value_in)
    back = value_in[:, 0, :]
    spread = jnp.concatenate(
        [jnp.where(iota((n_dev, slots), 0) // n_pair == h, back, 0.0) for h in range(n_group)], axis=1
    ).astype(bf16)
    w_t = dot(place[...], spread, 1, 1).astype(bf16)
    u = dot(w_t, hid[...], 0, 0)
    per = width // n_dev
    for b in range(width // 128):
        u_wide[:, b, :] = u[:, b * 128 : (b + 1) * 128]
    u_wide[:, width // 128 :, :] = u.T.reshape(n_dev, per, 128)
    u_out[...] = u_wide[...].astype(bf16)
    send_all(5, lambda group, pair: u_out.at[group * n_pair + pair], u_in)
    tile = 256
    for i in range(rows // tile):
        hg_ref[i * tile : (i + 1) * tile, :] = dot(w_t[i * tile : (i + 1) * tile], pq, 1, 0).astype(bf16)
    all_here(5, u_in)
    total = jnp.sum(u_in[...].astype(f32), axis=0) * inv_root
    n_b = width // 128
    u_row, u_col = total[:n_b], total[n_b:]
    wide = jnp.concatenate(
        [jnp.where(iota((n_b, 128), 0) == b, u_row, 0.0) for b in range(n_b)], axis=1
    )
    w_hi, w_lo = halves(wide)
    query_grad = dot(jnp.concatenate([w_hi, w_lo], axis=0), proj[...], 1, 0)
    qg_ref[...] = jnp.sum(query_grad, axis=0, keepdims=True)
    c_hi, c_lo = halves(u_col)
    proj_grad = dot(jnp.concatenate([c_hi, c_lo], axis=0), q_flat, 1, 0)
    pg_ref[...] = proj_grad[:per] + proj_grad[per:]

    part = q_all.at[pl.ds(0, n_group - 1)]
    pltpu.make_async_copy(part, part, send_sem.at[0]).wait()
    all_sent(1, req_in, n_dev - 1)
    all_sent(2, key_in, n_pair - 1)
    all_sent(3, score_in, n_dev - 1)
    all_sent(4, value_in, n_dev - 1)
    all_sent(5, u_in, n_dev - 1)


def finish_kernel(parts, hg_ref, loss_ref, qg_ref, pg_ref, hg_out, loss_out, qg_out, pg_out, loss_one, sem):
    loss_one[...] = loss_ref[:, 0:1]
    tile = hg_ref.shape[0] // parts
    stores = [
        pltpu.make_async_copy(source, target, sem.at[parts + n])
        for n, (source, target) in enumerate([(loss_one, loss_out), (qg_ref, qg_out), (pg_ref, pg_out)])
    ] + [
        pltpu.make_async_copy(
            hg_ref.at[pl.ds(i * tile, tile)], hg_out.at[pl.ds(i * tile, tile)], sem.at[i]
        )
        for i in range(parts)
    ]
    for store in stores:
        store.start()
    for store in stores:
        store.wait()


def shards(query_embed, teacher_scores, pair_owner, pair_row, passage_hidden, projection):
    width = query_embed.shape[2]
    q_rows = query_embed.shape[1]
    cand = teacher_scores.shape[3]
    n_pair, n_group = lax.axis_size("pair"), lax.axis_size("group")
    n_dev = n_pair * n_group
    cap = max(2, 2 * q_rows * cand // n_dev)
    slots = n_pair * cap
    k_all = cand * n_pair
    queries_n = n_group * q_rows
    rows = passage_hidden.shape[0]
    per = width // n_dev
    vmem = pl.BlockSpec(memory_space=pltpu.VMEM)
    hbm = pl.BlockSpec(memory_space=pltpu.HBM)
    message = pltpu.VMEM((n_dev, 1, slots), f32)
    results = pl.pallas_call(
        functools.partial(step_kernel, n_group, n_pair, cap),
        out_shape=(
            pltpu.VMEM((rows, width), bf16),
            pltpu.VMEM((1, 128), f32),
            pltpu.VMEM((1, width), f32),
            pltpu.VMEM((per, width), f32),
        ),
        in_specs=[hbm] * 6,
        out_specs=(vmem,) * 4,
        scratch_shapes=[
            pltpu.VMEM((q_rows, width), bf16),
            pltpu.VMEM((q_rows, cand), f32),
            pltpu.VMEM((q_rows, cand), i32),
            pltpu.VMEM((q_rows, cand), i32),
            pltpu.VMEM((rows, width), bf16),
            pltpu.VMEM((width, width), bf16),
            pltpu.VMEM((n_group, q_rows, width), bf16),
            message,
            message,
            pltpu.VMEM((q_rows, 1, 128), f32),
            pltpu.VMEM((n_pair, 1, 128), f32),
            pltpu.VMEM((n_group, 1, slots), f32),
            message,
            message,
            message,
            pltpu.VMEM((rows, n_group * slots), bf16),
            pltpu.VMEM((k_all, k_all), f32),
            pltpu.VMEM((n_dev, 16, 128), f32),
            pltpu.VMEM((n_dev, 16, 128), bf16),
            pltpu.VMEM((n_dev, 16, 128), bf16),
            pltpu.SemaphoreType.DMA((6,)),
            pltpu.SemaphoreType.DMA((6,)),
            pltpu.SemaphoreType.DMA((6,)),
        ],
        compiler_params=pltpu.CompilerParams(
            collective_id=0, has_side_effects=True, vmem_limit_bytes=44 * 2**20
        ),
        name="step",
    )(
        *(
            pltpu.with_memory_space_constraint(x, pltpu.HBM)
            for x in (
                query_embed[0],
                teacher_scores.reshape(q_rows, cand),
                pair_owner.reshape(q_rows, cand),
                pair_row.reshape(q_rows, cand),
                passage_hidden,
                projection,
            )
        )
    )
    parts = 8
    hidden_grad, loss, query_grad, projection_grad = pl.pallas_call(
        functools.partial(finish_kernel, parts),
        out_shape=(
            jax.ShapeDtypeStruct((rows, width), bf16),
            jax.ShapeDtypeStruct((1, 1), f32),
            jax.ShapeDtypeStruct((1, width), f32),
            jax.ShapeDtypeStruct((per, width), f32),
        ),
        in_specs=[vmem] * 4,
        out_specs=(hbm,) * 4,
        scratch_shapes=[pltpu.VMEM((1, 1), f32), pltpu.SemaphoreType.DMA((parts + 3,))],
        compiler_params=pltpu.CompilerParams(vmem_limit_bytes=4 * 2**20),
        name="finish",
    )(*results)
    return loss, query_grad.reshape(1, 1, width), hidden_grad, projection_grad


def solution(mesh):
    placed = (
        P("group", None, None),
        P("group", "pair", None, None),
        P("group", "pair", None, None, None),
        P("group", "pair", None, None),
        P(("group", "pair"), None),
        P(),
    )
    return jax.shard_map(
        shards,
        mesh=mesh,
        in_specs=placed,
        out_specs=(
            P("group", "pair"),
            P("group", "pair", None),
            P(("group", "pair"), None),
            P(("group", "pair"), None),
        ),
        check_vma=False,
    )
```

```python
import functools
import math

import jax
import jax.numpy as jnp
from jax import lax
from jax.experimental import pallas as pl
from jax.experimental.pallas import tpu as pltpu
from jax.sharding import PartitionSpec as P

MESH = pl.DeviceIdType.MESH
loss_scale = 1024.0
f32, bf16, i32 = jnp.float32, jnp.bfloat16, jnp.int32


def iota(shape, dim):
    return lax.broadcasted_iota(i32, shape, dim)


def dot(a, b, ca, cb):
    return lax.dot_general(a, b, (((ca,), (cb,)), ((), ())), preferred_element_type=f32)


def halves(x):
    high = x.astype(bf16)
    return high, (x - high.astype(f32)).astype(bf16)


def flat_row(x):
    return jnp.concatenate([x[i : i + 1, :] for i in range(x.shape[0])], axis=1)


def step_kernel(
    n_group, n_pair, n_core, side, cap,
    q_hbm, teach_hbm, owner_hbm, row_hbm, hid_hbm, proj_hbm,
    hg_ref, loss_ref, qg_ref, pg_ref,
    q_ref, teach_ref, owner_ref, row_ref,
    hid, proj, q_all, req_out, req_in, key_out, key_in, score_out, score_in,
    value_out, value_in, place, tanh_s, s_hi, s_lo, w_ref, u_ref, u_wide, u_there, u_here, u_out, u_in,
    load_sem, send_sem, recv_sem, plane_sem,
):
    n_dev = n_group * n_pair
    q_rows, width = q_ref.shape
    cand = teach_ref.shape[1]
    n_own = q_rows * cand
    k_all = cand * n_pair
    slots = n_pair * cap
    rows = hid.shape[0]
    den = float(k_all * (k_all * k_all - 1))
    inv_root = 1.0 / math.sqrt(width)
    g, r = lax.axis_index("group"), lax.axis_index("pair")
    me = g * n_pair + r
    n_plane = n_group // n_core
    in_plane = n_core * n_pair
    q_plane = n_core * q_rows
    s_plane = n_core * slots
    half = n_dev // n_core

    loads = [
        pltpu.make_async_copy(source, target, load_sem.at[n])
        for n, (source, target) in enumerate(
            [(owner_hbm, owner_ref), (row_hbm, row_ref), (teach_hbm, teach_ref), (q_hbm, q_ref),
             (proj_hbm, proj), (hid_hbm, hid)]
        )
    ]
    for load in loads:
        load.start()

    z, c = g // n_core, lax.rem(g, n_core)
    y, x = r // side, lax.rem(r, side)
    planes = sorted(range(n_plane), key=lambda d: -min(d, n_plane - d))
    steps = sorted(range(side), key=lambda d: -min(d, side - d))
    near = [(dy, dx) for dy in steps for dx in steps]
    near.sort(key=lambda d: -sum(min(v, side - v) for v in d))
    y_at = {d: lax.rem(y + d, side) * side for d in steps}
    x_at = {d: lax.rem(x + d, side) for d in steps}
    pairs = [y_at[dy] + x_at[dx] for dy, dx in near]
    z_at = {d: lax.rem(z + d, n_plane) for d in planes}

    def plane_peers(dz, visit):
        if dz:
            def both(i, carry):
                for pair in pairs:
                    visit(z_at[dz] * n_core + i, pair)
                return carry

            lax.fori_loop(0, n_core, both, 0)
        else:
            def partners(i, carry):
                for pair in pairs:
                    visit(z * n_core + lax.rem(c + i, n_core), pair)
                return carry

            lax.fori_loop(1, n_core, partners, 0)
            for pair in pairs[:-1]:
                visit(g, pair)

    barrier = pltpu.get_barrier_semaphore()

    def greet(group, pair):
        pl.semaphore_signal(
            barrier, inc=1, device_id={"group": group, "pair": pair}, device_id_type=MESH
        )

    for dz in planes:
        plane_peers(dz, greet)

    def send_plane(dz, send, recv, source_of, target, at):
        def one(group, pair):
            pltpu.make_async_remote_copy(
                src_ref=source_of(group, pair),
                dst_ref=target.at[at],
                send_sem=send,
                recv_sem=recv,
                device_id={"group": group, "pair": pair},
                device_id_type=MESH,
            ).start()

        plane_peers(dz, one)
        if dz == 0:
            pltpu.make_async_copy(source_of(g, r), target.at[at], recv).start()

    def index_of(group, pair):
        return group * n_pair + pair

    def all_here(number, target):
        pltpu.make_async_copy(target, target, recv_sem.at[number]).wait()

    def all_sent(number, target, count):
        part = target.at[pl.ds(0, count)]
        pltpu.make_async_copy(part, part, send_sem.at[number]).wait()

    for load in loads[:3]:
        load.wait()
    own, row = flat_row(owner_ref[...]), flat_row(row_ref[...])
    lane = iota((1, n_own), 1)
    hot = iota((n_dev, n_own), 0) == own
    hot_f = jnp.where(hot, 1.0, 0.0)
    hot_b = hot_f.astype(bf16)
    before = jnp.where(iota((n_own, n_own), 0) < iota((n_own, n_own), 1), 1.0, 0.0).astype(bf16)
    seen = dot(hot_b, before, 1, 0)
    slot = jnp.sum(hot_f * seen, axis=0, keepdims=True).astype(i32)
    at_slot = iota((slots, n_own), 0) == slot + r * cap
    high = ((row >> 4) + 1).astype(f32)
    low = ((row & 15) * 16 + lane // cand).astype(f32)
    req = dot(hot_b, jnp.where(at_slot, high, 0.0).astype(bf16), 1, 1) * 256.0 + dot(
        hot_b, jnp.where(at_slot, low, 0.0).astype(bf16), 1, 1
    )
    req_out[:, 0, :] = req
    tag = (own * cap + slot).astype(f32)
    for q in range(q_rows):
        key_out[q, :, 0:cand] = tag[:, q * cand : (q + 1) * cand]
        key_out[q, :, cand : 2 * cand] = teach_ref[q : q + 1, :]

    loads[3].wait()
    pl.semaphore_wait(barrier, n_dev - 1)

    def send_q(i, carry):
        other = lax.rem(g + i, n_group)
        pltpu.make_async_remote_copy(
            src_ref=q_ref,
            dst_ref=q_all.at[g],
            send_sem=send_sem.at[0],
            recv_sem=recv_sem.at[0],
            device_id={"group": other, "pair": r},
            device_id_type=MESH,
        ).start()
        return carry

    lax.fori_loop(1, n_group, send_q, 0, unroll=True)
    pltpu.make_async_copy(q_ref, q_all.at[g], recv_sem.at[0]).start()
    for dz in planes:
        send_plane(dz, send_sem.at[1], recv_sem.at[1], lambda *p: req_out.at[index_of(*p)], req_in, me)

    def send_key(i, carry):
        other = lax.rem(r + i, n_pair)
        pltpu.make_async_remote_copy(
            src_ref=key_out.at[other],
            dst_ref=key_in.at[r],
            send_sem=send_sem.at[2],
            recv_sem=recv_sem.at[2],
            device_id={"group": g, "pair": other},
            device_id_type=MESH,
        ).start()
        return carry

    lax.fori_loop(1, n_pair, send_key, 0, unroll=True)
    pltpu.make_async_copy(key_out.at[r], key_in.at[r], recv_sem.at[2]).start()

    all_here(0, q_all)
    loads[4].wait()
    queries_n = n_group * q_rows
    q_flat = q_all[...].reshape(queries_n, width)
    pq = (dot(q_flat, proj[...], 1, 1) * inv_root).astype(bf16)
    loads[5].wait()
    s_t = dot(pq, hid[...], 1, 1)
    s_hi[...], s_lo[...] = halves(s_t)

    all_here(1, req_in)
    of_group = iota((1, s_plane), 1) // slots
    for n, dz in enumerate(planes):
        asked = req_in[pl.ds(z_at[dz] * in_plane, in_plane)].reshape(n_core, n_pair, 1, slots)
        asked = jnp.sum(asked, axis=1).astype(i32)
        here = jnp.concatenate([asked[i] for i in range(n_core)], axis=1)
        mark = jnp.where(iota((rows, s_plane), 0) == (here >> 4) - 16, 1.0, 0.0).astype(bf16)
        place[n] = mark
        of_plane = pl.ds(pl.multiple_of(z_at[dz] * q_plane, q_plane), q_plane)
        picks = dot(jnp.concatenate([s_hi[of_plane, :], s_lo[of_plane, :]], axis=0), mark, 1, 0)
        picks = picks[:q_plane] + picks[q_plane:]
        of_query = (here & 15) + q_rows * of_group
        value = jnp.sum(
            jnp.where(iota((q_plane, s_plane), 0) == of_query, picks, 0.0), axis=0, keepdims=True
        )
        for i in range(n_core):
            score_out[z_at[dz] * n_core + i] = value[:, i * slots : (i + 1) * slots]
        send_plane(dz, send_sem.at[3], recv_sem.at[3], lambda group, pair: score_out.at[group], score_in, me)

    all_here(2, key_in)
    keys = key_in[:, 0, :]
    tags = flat_row(keys[:, 0:cand]).astype(i32)
    teach = flat_row(keys[:, cand : 2 * cand])
    k_owner = jnp.where(iota((n_dev, k_all), 0) == tags // cap, 1.0, 0.0).astype(bf16)
    k_slot = jnp.where(
        iota((slots, k_all), 0) == tags % cap + cap * (iota((1, k_all), 1) // cand), 1.0, 0.0
    )

    def column(x):
        return jnp.broadcast_to(x, (128, k_all)).T

    blocks = [(j * 128, (j + 1) * 128) for j in range(k_all // 128)]
    t_col = column(teach)
    t_sum = jnp.concatenate(
        [jnp.sum(jnp.tanh(t_col - teach[:, a:b]), axis=0, keepdims=True) for a, b in blocks], axis=1
    )
    all_here(3, score_in)
    t_hi, t_lo = halves(score_in[:, 0, :].T)
    picked = dot(jnp.concatenate([t_hi, t_lo], axis=0), k_owner, 1, 0)
    s_k = jnp.sum((picked[:slots] + picked[slots:]) * k_slot, axis=0, keepdims=True)
    s_col = column(s_k)
    sums = []
    for a, b in blocks:
        soft = jnp.tanh(s_col - s_k[:, a:b])
        tanh_s[:, a:b] = soft
        sums.append(jnp.sum(soft, axis=0, keepdims=True))
    gap = 0.5 * (jnp.concatenate(sums, axis=1) - t_sum)
    loss_ref[...] = jnp.broadcast_to(6.0 * jnp.sum(gap * gap, axis=1, keepdims=True) / den, (1, 128))
    grad = gap * (loss_scale * 12.0 / den)
    g_col = column(grad)
    parts = []
    for a, b in blocks:
        soft = tanh_s[:, a:b]
        parts.append(
            jnp.sum((g_col - grad[:, a:b]) * (1.0 - soft * soft), axis=0, keepdims=True)
        )
    s_grad = 0.5 * jnp.concatenate(parts, axis=1)
    value_out[:, 0, :] = dot(k_owner, (k_slot * s_grad).astype(bf16), 1, 1)
    for dz in planes:
        send_plane(
            dz, send_sem.at[4], plane_sem.at[(n_plane - dz) % n_plane],
            lambda *p: value_out.at[index_of(*p)], value_in, me,
        )

    row_of = iota((in_plane, slots), 0) // n_pair
    for n, dz in reversed(list(enumerate(planes))):
        arrived = value_in.at[pl.ds(z_at[dz] * in_plane, in_plane)]
        pltpu.make_async_copy(arrived, arrived, plane_sem.at[dz]).wait()
        back = value_in[pl.ds(z_at[dz] * in_plane, in_plane), 0, :]
        spread = jnp.concatenate([jnp.where(row_of == i, back, 0.0) for i in range(n_core)], axis=1)
        of_plane = pl.ds(pl.multiple_of(z_at[dz] * q_plane, q_plane), q_plane)
        w_ref[of_plane, :] = dot(spread.astype(bf16), place[n], 1, 1).astype(bf16)
    u_ref[...] = dot(w_ref[...], hid[...], 1, 0).reshape(n_group, q_rows, width)
    per = width // n_dev
    n_b = width // 128

    def gather_half(core):
        for plane in range(n_plane):
            group = plane * n_core + core
            of_rows = u_ref[group]
            for b in range(n_b):
                u_wide[plane * n_pair : (plane + 1) * n_pair, b, :] = of_rows[:, b * 128 : (b + 1) * 128]
            width_group = n_pair * per
            lanes = pl.ds(pl.multiple_of(group * width_group, width_group), width_group)
            columns = u_ref[:, :, lanes].reshape(n_dev, width_group)
            u_wide[plane * n_pair : (plane + 1) * n_pair, n_b:, :] = columns.T.reshape(n_pair, per, n_dev)

    partner = lax.rem(c + 1, n_core)
    gather_half(partner)
    u_there[...] = u_wide[...].astype(bf16)
    to_partner = pltpu.make_async_remote_copy(
        src_ref=u_there,
        dst_ref=u_here,
        send_sem=send_sem.at[6],
        recv_sem=recv_sem.at[6],
        device_id={"group": z * n_core + partner, "pair": r},
        device_id_type=MESH,
    )
    to_partner.start()
    gather_half(c)
    to_partner.wait_recv()
    u_out[...] = (u_wide[...] + u_here[...].astype(f32)).astype(bf16)
    at = z * n_pair + r

    def send_u(plane, pair):
        pltpu.make_async_remote_copy(
            src_ref=u_out.at[plane * n_pair + pair],
            dst_ref=u_in.at[at],
            send_sem=send_sem.at[5],
            recv_sem=recv_sem.at[5],
            device_id={"group": plane * n_core + c, "pair": pair},
            device_id_type=MESH,
        ).start()

    for dz in planes:
        for pair in pairs if dz else pairs[:-1]:
            send_u(z_at[dz], pair)
    pltpu.make_async_copy(u_out.at[at], u_in.at[at], recv_sem.at[5]).start()
    w_t = w_ref[...].T
    tile = 256
    for i in range(rows // tile):
        hg_ref[i * tile : (i + 1) * tile, :] = dot(w_t[i * tile : (i + 1) * tile], pq, 1, 0).astype(bf16)
    all_here(5, u_in)
    total = jnp.sum(u_in[...].astype(f32), axis=0) * inv_root
    u_row, u_col = total[:n_b], total[n_b:]
    wide = jnp.concatenate(
        [jnp.where(iota((n_b, 128), 0) == b, u_row, 0.0) for b in range(n_b)], axis=1
    )
    w_hi, w_lo = halves(wide)
    query_grad = dot(jnp.concatenate([w_hi, w_lo], axis=0), proj[...], 1, 0)
    qg_ref[...] = jnp.sum(query_grad, axis=0, keepdims=True)
    c_hi, c_lo = halves(u_col)
    proj_grad = dot(jnp.concatenate([c_hi, c_lo], axis=0), q_flat, 1, 0)
    pg_ref[...] = proj_grad[:per] + proj_grad[per:]

    part = q_all.at[pl.ds(0, n_group - 1)]
    pltpu.make_async_copy(part, part, send_sem.at[0]).wait()
    all_sent(1, req_in, n_dev - 1)
    all_sent(2, key_in, n_pair - 1)
    all_sent(3, score_in, n_dev - 1)
    all_sent(4, value_in, n_dev - 1)
    all_sent(5, u_in, half - 1)
    to_partner.wait_send()


def finish_kernel(parts, hg_ref, loss_ref, qg_ref, pg_ref, hg_out, loss_out, qg_out, pg_out, loss_one, sem):
    loss_one[...] = loss_ref[:, 0:1]
    tile = hg_ref.shape[0] // parts
    stores = [
        pltpu.make_async_copy(source, target, sem.at[parts + n])
        for n, (source, target) in enumerate([(loss_one, loss_out), (qg_ref, qg_out), (pg_ref, pg_out)])
    ] + [
        pltpu.make_async_copy(
            hg_ref.at[pl.ds(i * tile, tile)], hg_out.at[pl.ds(i * tile, tile)], sem.at[i]
        )
        for i in range(parts)
    ]
    for store in stores:
        store.start()
    for store in stores:
        store.wait()


def shards(query_embed, teacher_scores, pair_owner, pair_row, passage_hidden, projection):
    width = query_embed.shape[2]
    q_rows = query_embed.shape[1]
    cand = teacher_scores.shape[3]
    n_pair, n_group = lax.axis_size("pair"), lax.axis_size("group")
    n_dev = n_pair * n_group
    cap = max(2, 2 * q_rows * cand // n_dev)
    slots = n_pair * cap
    k_all = cand * n_pair
    queries_n = n_group * q_rows
    n_core, side = 2, math.isqrt(n_pair)
    rows = passage_hidden.shape[0]
    per = width // n_dev
    vmem = pl.BlockSpec(memory_space=pltpu.VMEM)
    hbm = pl.BlockSpec(memory_space=pltpu.HBM)
    message = pltpu.VMEM((n_dev, 1, slots), f32)
    results = pl.pallas_call(
        functools.partial(step_kernel, n_group, n_pair, n_core, side, cap),
        out_shape=(
            pltpu.VMEM((rows, width), bf16),
            pltpu.VMEM((1, 128), f32),
            pltpu.VMEM((1, width), f32),
            pltpu.VMEM((per, width), f32),
        ),
        in_specs=[hbm] * 6,
        out_specs=(vmem,) * 4,
        scratch_shapes=[
            pltpu.VMEM((q_rows, width), bf16),
            pltpu.VMEM((q_rows, cand), f32),
            pltpu.VMEM((q_rows, cand), i32),
            pltpu.VMEM((q_rows, cand), i32),
            pltpu.VMEM((rows, width), bf16),
            pltpu.VMEM((width, width), bf16),
            pltpu.VMEM((n_group, q_rows, width), bf16),
            message,
            message,
            pltpu.VMEM((q_rows, 1, 128), f32),
            pltpu.VMEM((n_pair, 1, 128), f32),
            pltpu.VMEM((n_group, 1, slots), f32),
            message,
            message,
            message,
            pltpu.VMEM((n_group // n_core, rows, n_core * slots), bf16),
            pltpu.VMEM((k_all, k_all), f32),
            pltpu.VMEM((queries_n, rows), bf16),
            pltpu.VMEM((queries_n, rows), bf16),
            pltpu.VMEM((queries_n, rows), bf16),
            pltpu.VMEM((n_group, q_rows, width), f32),
            pltpu.VMEM((n_dev // n_core, 16, 128), f32),
            pltpu.VMEM((n_dev // n_core, 16, 128), bf16),
            pltpu.VMEM((n_dev // n_core, 16, 128), bf16),
            pltpu.VMEM((n_dev // n_core, 16, 128), bf16),
            pltpu.VMEM((n_dev // n_core, 16, 128), bf16),
            pltpu.SemaphoreType.DMA((6,)),
            pltpu.SemaphoreType.DMA((7,)),
            pltpu.SemaphoreType.DMA((7,)),
            pltpu.SemaphoreType.DMA((n_group // n_core,)),
        ],
        compiler_params=pltpu.CompilerParams(
            collective_id=0, has_side_effects=True, vmem_limit_bytes=44 * 2**20
        ),
        name="step",
    )(
        *(
            pltpu.with_memory_space_constraint(x, pltpu.HBM)
            for x in (
                query_embed[0],
                teacher_scores.reshape(q_rows, cand),
                pair_owner.reshape(q_rows, cand),
                pair_row.reshape(q_rows, cand),
                passage_hidden,
                projection,
            )
        )
    )
    parts = 8
    hidden_grad, loss, query_grad, projection_grad = pl.pallas_call(
        functools.partial(finish_kernel, parts),
        out_shape=(
            jax.ShapeDtypeStruct((rows, width), bf16),
            jax.ShapeDtypeStruct((1, 1), f32),
            jax.ShapeDtypeStruct((1, width), f32),
            jax.ShapeDtypeStruct((per, width), f32),
        ),
        in_specs=[vmem] * 4,
        out_specs=(hbm,) * 4,
        scratch_shapes=[pltpu.VMEM((1, 1), f32), pltpu.SemaphoreType.DMA((parts + 3,))],
        compiler_params=pltpu.CompilerParams(vmem_limit_bytes=4 * 2**20),
        name="finish",
    )(*results)
    return loss, query_grad.reshape(1, 1, width), hidden_grad, projection_grad


def solution(mesh):
    placed = (
        P("group", None, None),
        P("group", "pair", None, None),
        P("group", "pair", None, None, None),
        P("group", "pair", None, None),
        P(("group", "pair"), None),
        P(),
    )
    return jax.shard_map(
        shards,
        mesh=mesh,
        in_specs=placed,
        out_specs=(
            P("group", "pair"),
            P("group", "pair", None),
            P(("group", "pair"), None),
            P(("group", "pair"), None),
        ),
        check_vma=False,
    )
```

```python
import functools
import math

import jax
import jax.numpy as jnp
from jax import lax
from jax.experimental import pallas as pl
from jax.experimental.pallas import tpu as pltpu
from jax.sharding import PartitionSpec as P

MESH = pl.DeviceIdType.MESH
loss_scale = 1024.0
f32, bf16, i32 = jnp.float32, jnp.bfloat16, jnp.int32


def iota(shape, dim):
    return lax.broadcasted_iota(i32, shape, dim)


def dot(a, b, ca, cb):
    return lax.dot_general(a, b, (((ca,), (cb,)), ((), ())), preferred_element_type=f32)


def halves(x):
    high = x.astype(bf16)
    return high, (x - high.astype(f32)).astype(bf16)


def flat_row(x):
    return jnp.concatenate([x[i : i + 1, :] for i in range(x.shape[0])], axis=1)


def step_kernel(
    n_group, n_pair, n_core, side, cap,
    q_hbm, teach_hbm, owner_hbm, row_hbm, hid_hbm, proj_hbm,
    hg_ref, loss_ref, qg_ref, pg_ref,
    q_ref, teach_ref, owner_ref, row_ref,
    hid, proj, pq_own, pq_all, q_all, req_out, req_in, key_out, key_in, score_out, score_in,
    value_out, value_in, place, tanh_s, s_hi, s_lo, w_ref, u_wide, u_there, u_here, u_out, u_in,
    load_sem, send_sem, recv_sem, plane_sem,
):
    n_dev = n_group * n_pair
    q_rows, width = q_ref.shape
    cand = teach_ref.shape[1]
    n_own = q_rows * cand
    k_all = cand * n_pair
    slots = n_pair * cap
    rows = hid.shape[0]
    den = float(k_all * (k_all * k_all - 1))
    inv_root = 1.0 / math.sqrt(width)
    g, r = lax.axis_index("group"), lax.axis_index("pair")
    me = g * n_pair + r
    n_plane = n_group // n_core
    in_plane = n_core * n_pair
    q_plane = n_core * q_rows
    s_plane = n_core * slots
    half = n_dev // n_core

    loads = [
        pltpu.make_async_copy(source, target, load_sem.at[n])
        for n, (source, target) in enumerate(
            [(owner_hbm, owner_ref), (row_hbm, row_ref), (teach_hbm, teach_ref), (q_hbm, q_ref),
             (proj_hbm, proj), (hid_hbm, hid)]
        )
    ]
    for load in loads:
        load.start()

    z, c = g // n_core, lax.rem(g, n_core)
    y, x = r // side, lax.rem(r, side)
    planes = sorted(range(n_plane), key=lambda d: -min(d, n_plane - d))
    steps = sorted(range(side), key=lambda d: -min(d, side - d))
    near = [(dy, dx) for dy in steps for dx in steps]
    near.sort(key=lambda d: -sum(min(v, side - v) for v in d))
    y_at = {d: lax.rem(y + d, side) * side for d in steps}
    x_at = {d: lax.rem(x + d, side) for d in steps}
    pairs = [y_at[dy] + x_at[dx] for dy, dx in near]
    z_at = {d: lax.rem(z + d, n_plane) for d in planes}

    def plane_peers(dz, visit):
        if dz:
            def both(i, carry):
                for pair in pairs:
                    visit(z_at[dz] * n_core + i, pair)
                return carry

            lax.fori_loop(0, n_core, both, 0)
        else:
            def partners(i, carry):
                for pair in pairs:
                    visit(z * n_core + lax.rem(c + i, n_core), pair)
                return carry

            lax.fori_loop(1, n_core, partners, 0)
            for pair in pairs[:-1]:
                visit(g, pair)

    barrier = pltpu.get_barrier_semaphore()

    def greet(group, pair):
        pl.semaphore_signal(
            barrier, inc=1, device_id={"group": group, "pair": pair}, device_id_type=MESH
        )

    for dz in planes:
        plane_peers(dz, greet)

    def send_plane(dz, send, recv, source_of, target, at):
        def one(group, pair):
            pltpu.make_async_remote_copy(
                src_ref=source_of(group, pair),
                dst_ref=target.at[at],
                send_sem=send,
                recv_sem=recv,
                device_id={"group": group, "pair": pair},
                device_id_type=MESH,
            ).start()

        plane_peers(dz, one)
        if dz == 0:
            pltpu.make_async_copy(source_of(g, r), target.at[at], recv).start()

    def index_of(group, pair):
        return group * n_pair + pair

    def all_here(number, target):
        pltpu.make_async_copy(target, target, recv_sem.at[number]).wait()

    def all_sent(number, target, count):
        part = target.at[pl.ds(0, count)]
        pltpu.make_async_copy(part, part, send_sem.at[number]).wait()

    for load in loads[:3]:
        load.wait()
    own, row = flat_row(owner_ref[...]), flat_row(row_ref[...])
    lane = iota((1, n_own), 1)
    hot = iota((n_dev, n_own), 0) == own
    hot_f = jnp.where(hot, 1.0, 0.0)
    hot_b = hot_f.astype(bf16)
    before = jnp.where(iota((n_own, n_own), 0) < iota((n_own, n_own), 1), 1.0, 0.0).astype(bf16)
    seen = dot(hot_b, before, 1, 0)
    slot = jnp.sum(hot_f * seen, axis=0, keepdims=True).astype(i32)
    at_slot = iota((slots, n_own), 0) == slot + r * cap
    high = ((row >> 4) + 1).astype(f32)
    low = ((row & 15) * 16 + lane // cand).astype(f32)
    req = dot(hot_b, jnp.where(at_slot, high, 0.0).astype(bf16), 1, 1) * 256.0 + dot(
        hot_b, jnp.where(at_slot, low, 0.0).astype(bf16), 1, 1
    )
    req_out[:, 0, :] = req
    tag = (own * cap + slot).astype(f32)
    for q in range(q_rows):
        key_out[q, :, 0:cand] = tag[:, q * cand : (q + 1) * cand]
        key_out[q, :, cand : 2 * cand] = teach_ref[q : q + 1, :]

    loads[3].wait()
    loads[4].wait()
    pq_own[...] = (dot(q_ref[...], proj[...], 1, 1) * inv_root).astype(bf16)

    pl.semaphore_wait(barrier, n_dev - 1)

    partner = lax.rem(c + 1, n_core)
    there = {"group": z * n_core + partner, "pair": r}

    few = q_all.at[pl.ds(0, n_plane)]

    def spread_rows(source, target, first, second):
        def send(what, group, sem, where):
            pltpu.make_async_remote_copy(
                src_ref=what,
                dst_ref=target.at[group],
                send_sem=send_sem.at[sem],
                recv_sem=recv_sem.at[sem],
                device_id=where,
                device_id_type=MESH,
            ).start()

        for dz in planes[:-1]:
            send(source, g, first, {"group": z_at[dz] * n_core + c, "pair": r})
        send(source, g, second, there)
        pltpu.make_async_copy(source, target.at[g], recv_sem.at[first]).start()

        def forward():
            pltpu.make_async_copy(few, few, recv_sem.at[first]).wait()
            for dz in planes[:-1]:
                group = z_at[dz] * n_core + c
                send(target.at[group], group, second, there)

        return forward

    forward_pq = spread_rows(pq_own, pq_all, 0, 7)
    for dz in planes:
        send_plane(dz, send_sem.at[1], recv_sem.at[1], lambda *p: req_out.at[index_of(*p)], req_in, me)

    def send_key(i, carry):
        other = lax.rem(r + i, n_pair)
        pltpu.make_async_remote_copy(
            src_ref=key_out.at[other],
            dst_ref=key_in.at[r],
            send_sem=send_sem.at[2],
            recv_sem=recv_sem.at[2],
            device_id={"group": g, "pair": other},
            device_id_type=MESH,
        ).start()
        return carry

    lax.fori_loop(1, n_pair, send_key, 0, unroll=True)
    pltpu.make_async_copy(key_out.at[r], key_in.at[r], recv_sem.at[2]).start()

    forward_pq()

    pltpu.make_async_copy(few, few, recv_sem.at[7]).wait()
    loads[5].wait()
    queries_n = n_group * q_rows
    pq = pq_all[...].reshape(queries_n, width)
    s_t = dot(pq, hid[...], 1, 1)
    s_hi[...], s_lo[...] = halves(s_t)

    all_here(1, req_in)
    of_group = iota((1, s_plane), 1) // slots
    for n, dz in enumerate(planes):
        asked = req_in[pl.ds(z_at[dz] * in_plane, in_plane)].reshape(n_core, n_pair, 1, slots)
        asked = jnp.sum(asked, axis=1).astype(i32)
        here = jnp.concatenate([asked[i] for i in range(n_core)], axis=1)
        wanted = jnp.broadcast_to((here >> 4) - 16, (16, s_plane)).astype(jnp.int16)
        wanted = jnp.broadcast_to(wanted[None], (rows // 16, 16, s_plane)).reshape(rows, s_plane)
        mark = jnp.where(iota((rows, s_plane), 0).astype(jnp.int16) == wanted, bf16(1.0), bf16(0.0))
        place[n] = mark
        of_plane = pl.ds(pl.multiple_of(z_at[dz] * q_plane, q_plane), q_plane)
        picks = dot(jnp.concatenate([s_hi[of_plane, :], s_lo[of_plane, :]], axis=0), mark, 1, 0)
        picks = picks[:q_plane] + picks[q_plane:]
        of_query = (here & 15) + q_rows * of_group
        value = jnp.sum(
            jnp.where(iota((q_plane, s_plane), 0) == of_query, picks, 0.0), axis=0, keepdims=True
        )
        for i in range(n_core):
            score_out[z_at[dz] * n_core + i] = value[:, i * slots : (i + 1) * slots]
        send_plane(dz, send_sem.at[3], recv_sem.at[3], lambda group, pair: score_out.at[group], score_in, me)

    all_here(2, key_in)
    keys = key_in[:, 0, :]
    tags = flat_row(keys[:, 0:cand]).astype(i32)
    teach = flat_row(keys[:, cand : 2 * cand])
    k_owner = jnp.where(iota((n_dev, k_all), 0) == tags // cap, 1.0, 0.0).astype(bf16)
    k_slot = jnp.where(
        iota((slots, k_all), 0) == tags % cap + cap * (iota((1, k_all), 1) // cand), 1.0, 0.0
    )

    def column(x):
        return jnp.broadcast_to(x, (128, k_all)).T

    blocks = [(j * 128, (j + 1) * 128) for j in range(k_all // 128)]
    t_col = column(teach)
    t_sum = jnp.concatenate(
        [jnp.sum(jnp.tanh(t_col - teach[:, a:b]), axis=0, keepdims=True) for a, b in blocks], axis=1
    )
    all_here(3, score_in)
    forward_q = spread_rows(q_ref, q_all, 8, 9)
    t_hi, t_lo = halves(score_in[:, 0, :].T)
    picked = dot(jnp.concatenate([t_hi, t_lo], axis=0), k_owner, 1, 0)
    s_k = jnp.sum((picked[:slots] + picked[slots:]) * k_slot, axis=0, keepdims=True)
    s_col = column(s_k)
    sums = []
    for a, b in blocks:
        soft = jnp.tanh(s_col - s_k[:, a:b])
        tanh_s[:, a:b] = soft
        sums.append(jnp.sum(soft, axis=0, keepdims=True))
    gap = 0.5 * (jnp.concatenate(sums, axis=1) - t_sum)
    loss_ref[...] = jnp.broadcast_to(6.0 * jnp.sum(gap * gap, axis=1, keepdims=True) / den, (1, 128))
    grad = gap * (loss_scale * 12.0 / den)
    g_col = column(grad)
    parts = []
    for a, b in blocks:
        soft = tanh_s[:, a:b]
        parts.append(
            jnp.sum((g_col - grad[:, a:b]) * (1.0 - soft * soft), axis=0, keepdims=True)
        )
    s_grad = 0.5 * jnp.concatenate(parts, axis=1)
    value_out[:, 0, :] = dot(k_owner, (k_slot * s_grad).astype(bf16), 1, 1)
    for dz in planes:
        send_plane(
            dz, send_sem.at[4], plane_sem.at[(n_plane - dz) % n_plane],
            lambda *p: value_out.at[index_of(*p)], value_in, me,
        )

    row_of = iota((in_plane, slots), 0) // n_pair
    for n, dz in reversed(list(enumerate(planes))):
        arrived = value_in.at[pl.ds(z_at[dz] * in_plane, in_plane)]
        pltpu.make_async_copy(arrived, arrived, plane_sem.at[dz]).wait()
        back = value_in[pl.ds(z_at[dz] * in_plane, in_plane), 0, :]
        spread = jnp.concatenate([jnp.where(row_of == i, back, 0.0) for i in range(n_core)], axis=1)
        of_plane = pl.ds(pl.multiple_of(z_at[dz] * q_plane, q_plane), q_plane)
        w_ref[of_plane, :] = dot(spread.astype(bf16), place[n], 1, 1).astype(bf16)
    per = width // n_dev
    n_b = width // 128
    width_group = n_pair * per
    width_plane = n_core * width_group
    for plane in range(n_plane):
        u = dot(w_ref[...], hid[:, plane * width_plane : (plane + 1) * width_plane], 1, 0)
        by_group = u.reshape(n_plane, n_core, q_rows, width_plane)
        for core in range(n_core):
            columns = u[:, core * width_group : (core + 1) * width_group]
            u_wide[core, plane * n_pair : (plane + 1) * n_pair, n_b:, :] = columns.T.reshape(n_pair, per, n_dev)
            for i in range(width_plane // 128):
                b = plane * (width_plane // 128) + i
                u_wide[core, :, b, :] = by_group[:, core, :, i * 128 : (i + 1) * 128].reshape(half, 128)

    u_there[...] = u_wide[partner].astype(bf16)
    to_partner = pltpu.make_async_remote_copy(
        src_ref=u_there,
        dst_ref=u_here,
        send_sem=send_sem.at[6],
        recv_sem=recv_sem.at[6],
        device_id=there,
        device_id_type=MESH,
    )
    to_partner.start()
    to_partner.wait_recv()
    u_out[...] = (u_wide[c] + u_here[...].astype(f32)).astype(bf16)
    at = z * n_pair + r

    def send_u(plane, pair):
        pltpu.make_async_remote_copy(
            src_ref=u_out.at[plane * n_pair + pair],
            dst_ref=u_in.at[at],
            send_sem=send_sem.at[5],
            recv_sem=recv_sem.at[5],
            device_id={"group": plane * n_core + c, "pair": pair},
            device_id_type=MESH,
        ).start()

    for dz in planes:
        for pair in pairs if dz else pairs[:-1]:
            send_u(z_at[dz], pair)
    pltpu.make_async_copy(u_out.at[at], u_in.at[at], recv_sem.at[5]).start()
    forward_q()
    w_t = w_ref[...].T
    tile = 256
    for i in range(rows // tile):
        hg_ref[i * tile : (i + 1) * tile, :] = dot(w_t[i * tile : (i + 1) * tile], pq, 1, 0).astype(bf16)
    all_here(5, u_in)
    total = jnp.sum(u_in[...].astype(f32), axis=0) * inv_root
    u_row, u_col = total[:n_b], total[n_b:]
    wide = jnp.concatenate(
        [jnp.where(iota((n_b, 128), 0) == b, u_row, 0.0) for b in range(n_b)], axis=1
    )
    w_hi, w_lo = halves(wide)
    query_grad = dot(jnp.concatenate([w_hi, w_lo], axis=0), proj[...], 1, 0)
    qg_ref[...] = jnp.sum(query_grad, axis=0, keepdims=True)
    c_hi, c_lo = halves(u_col)
    pltpu.make_async_copy(few, few, recv_sem.at[9]).wait()
    q_flat = q_all[...].reshape(queries_n, width)
    proj_grad = dot(jnp.concatenate([c_hi, c_lo], axis=0), q_flat, 1, 0)
    pg_ref[...] = proj_grad[:per] + proj_grad[per:]

    all_sent(0, q_all, n_plane - 1)
    all_sent(7, q_all, n_plane)
    all_sent(8, q_all, n_plane - 1)
    all_sent(9, q_all, n_plane)
    all_sent(1, req_in, n_dev - 1)
    all_sent(2, key_in, n_pair - 1)
    all_sent(3, score_in, n_dev - 1)
    all_sent(4, value_in, n_dev - 1)
    all_sent(5, u_in, half - 1)
    to_partner.wait_send()


def finish_kernel(parts, hg_ref, loss_ref, qg_ref, pg_ref, hg_out, loss_out, qg_out, pg_out, loss_one, sem):
    loss_one[...] = loss_ref[:, 0:1]
    tile = hg_ref.shape[0] // parts
    stores = [
        pltpu.make_async_copy(source, target, sem.at[parts + n])
        for n, (source, target) in enumerate([(loss_one, loss_out), (qg_ref, qg_out), (pg_ref, pg_out)])
    ] + [
        pltpu.make_async_copy(
            hg_ref.at[pl.ds(i * tile, tile)], hg_out.at[pl.ds(i * tile, tile)], sem.at[i]
        )
        for i in range(parts)
    ]
    for store in stores:
        store.start()
    for store in stores:
        store.wait()


def shards(query_embed, teacher_scores, pair_owner, pair_row, passage_hidden, projection):
    width = query_embed.shape[2]
    q_rows = query_embed.shape[1]
    cand = teacher_scores.shape[3]
    n_pair, n_group = lax.axis_size("pair"), lax.axis_size("group")
    n_dev = n_pair * n_group
    cap = max(2, 2 * q_rows * cand // n_dev)
    slots = n_pair * cap
    k_all = cand * n_pair
    queries_n = n_group * q_rows
    n_core, side = 2, math.isqrt(n_pair)
    rows = passage_hidden.shape[0]
    per = width // n_dev
    vmem = pl.BlockSpec(memory_space=pltpu.VMEM)
    hbm = pl.BlockSpec(memory_space=pltpu.HBM)
    message = pltpu.VMEM((n_dev, 1, slots), f32)
    results = pl.pallas_call(
        functools.partial(step_kernel, n_group, n_pair, n_core, side, cap),
        out_shape=(
            pltpu.VMEM((rows, width), bf16),
            pltpu.VMEM((1, 128), f32),
            pltpu.VMEM((1, width), f32),
            pltpu.VMEM((per, width), f32),
        ),
        in_specs=[hbm] * 6,
        out_specs=(vmem,) * 4,
        scratch_shapes=[
            pltpu.VMEM((q_rows, width), bf16),
            pltpu.VMEM((q_rows, cand), f32),
            pltpu.VMEM((q_rows, cand), i32),
            pltpu.VMEM((q_rows, cand), i32),
            pltpu.VMEM((rows, width), bf16),
            pltpu.VMEM((width, width), bf16),
            pltpu.VMEM((q_rows, width), bf16),
            pltpu.VMEM((n_group, q_rows, width), bf16),
            pltpu.VMEM((n_group, q_rows, width), bf16),
            message,
            message,
            pltpu.VMEM((q_rows, 1, 128), f32),
            pltpu.VMEM((n_pair, 1, 128), f32),
            pltpu.VMEM((n_group, 1, slots), f32),
            message,
            message,
            message,
            pltpu.VMEM((n_group // n_core, rows, n_core * slots), bf16),
            pltpu.VMEM((k_all, k_all), f32),
            pltpu.VMEM((queries_n, rows), bf16),
            pltpu.VMEM((queries_n, rows), bf16),
            pltpu.VMEM((queries_n, rows), bf16),
            pltpu.VMEM((n_core, n_dev // n_core, 16, 128), f32),
            pltpu.VMEM((n_dev // n_core, 16, 128), bf16),
            pltpu.VMEM((n_dev // n_core, 16, 128), bf16),
            pltpu.VMEM((n_dev // n_core, 16, 128), bf16),
            pltpu.VMEM((n_dev // n_core, 16, 128), bf16),
            pltpu.SemaphoreType.DMA((6,)),
            pltpu.SemaphoreType.DMA((10,)),
            pltpu.SemaphoreType.DMA((10,)),
            pltpu.SemaphoreType.DMA((n_group // n_core,)),
        ],
        compiler_params=pltpu.CompilerParams(
            collective_id=0, has_side_effects=True, vmem_limit_bytes=44 * 2**20
        ),
        name="step",
    )(
        *(
            pltpu.with_memory_space_constraint(x, pltpu.HBM)
            for x in (
                query_embed[0],
                teacher_scores.reshape(q_rows, cand),
                pair_owner.reshape(q_rows, cand),
                pair_row.reshape(q_rows, cand),
                passage_hidden,
                projection,
            )
        )
    )
    parts = 8
    hidden_grad, loss, query_grad, projection_grad = pl.pallas_call(
        functools.partial(finish_kernel, parts),
        out_shape=(
            jax.ShapeDtypeStruct((rows, width), bf16),
            jax.ShapeDtypeStruct((1, 1), f32),
            jax.ShapeDtypeStruct((1, width), f32),
            jax.ShapeDtypeStruct((per, width), f32),
        ),
        in_specs=[vmem] * 4,
        out_specs=(hbm,) * 4,
        scratch_shapes=[pltpu.VMEM((1, 1), f32), pltpu.SemaphoreType.DMA((parts + 3,))],
        compiler_params=pltpu.CompilerParams(vmem_limit_bytes=4 * 2**20),
        name="finish",
    )(*results)
    return loss, query_grad.reshape(1, 1, width), hidden_grad, projection_grad


def solution(mesh):
    placed = (
        P("group", None, None),
        P("group", "pair", None, None),
        P("group", "pair", None, None, None),
        P("group", "pair", None, None),
        P(("group", "pair"), None),
        P(),
    )
    return jax.shard_map(
        shards,
        mesh=mesh,
        in_specs=placed,
        out_specs=(
            P("group", "pair"),
            P("group", "pair", None),
            P(("group", "pair"), None),
            P(("group", "pair"), None),
        ),
        check_vma=False,
    )
```

```python
import functools
import math

import jax
import jax.numpy as jnp
from jax import lax
from jax.experimental import pallas as pl
from jax.experimental.pallas import tpu as pltpu
from jax.sharding import PartitionSpec as P

MESH = pl.DeviceIdType.MESH
loss_scale = 1024.0
f32, bf16, i32 = jnp.float32, jnp.bfloat16, jnp.int32


def iota(shape, dim):
    return lax.broadcasted_iota(i32, shape, dim)


def dot(a, b, ca, cb):
    return lax.dot_general(a, b, (((ca,), (cb,)), ((), ())), preferred_element_type=f32)


def halves(x):
    high = x.astype(bf16)
    return high, (x - high.astype(f32)).astype(bf16)


def flat_row(x):
    return jnp.concatenate([x[i : i + 1, :] for i in range(x.shape[0])], axis=1)


def step_kernel(
    n_group, n_pair, n_core, side, cap,
    q_hbm, teach_hbm, owner_hbm, row_hbm, hid_hbm, proj_hbm,
    hg_ref, loss_ref, total_ref, proj, q_out,
    q_ref, teach_ref, owner_ref, row_ref,
    hid, pq_own, pq_all, q_all, req_out, req_in, key_out, key_in, score_out, score_in,
    value_out, value_in, place, slopes, s_hi, s_lo, w_ref, u_wide, u_there, u_here, u_out, u_in,
    load_sem, send_sem, recv_sem, plane_sem,
):
    n_dev = n_group * n_pair
    q_rows, width = q_ref.shape
    cand = teach_ref.shape[1]
    n_own = q_rows * cand
    k_all = cand * n_pair
    slots = n_pair * cap
    rows = hid.shape[0]
    den = float(k_all * (k_all * k_all - 1))
    inv_root = 1.0 / math.sqrt(width)
    g, r = lax.axis_index("group"), lax.axis_index("pair")
    me = g * n_pair + r
    n_plane = n_group // n_core
    in_plane = n_core * n_pair
    q_plane = n_core * q_rows
    s_plane = n_core * slots
    half = n_dev // n_core

    loads = [
        pltpu.make_async_copy(source, target, load_sem.at[n])
        for n, (source, target) in enumerate(
            [(owner_hbm, owner_ref), (row_hbm, row_ref), (teach_hbm, teach_ref), (q_hbm, q_ref),
             (proj_hbm, proj), (hid_hbm, hid)]
        )
    ]
    for load in loads:
        load.start()

    z, c = g // n_core, lax.rem(g, n_core)
    y, x = r // side, lax.rem(r, side)
    planes = sorted(range(n_plane), key=lambda d: -min(d, n_plane - d))
    steps = sorted(range(side), key=lambda d: -min(d, side - d))
    near = [(dy, dx) for dy in steps for dx in steps]
    near.sort(key=lambda d: -sum(min(v, side - v) for v in d))
    y_at = {d: lax.rem(y + d, side) * side for d in steps}
    x_at = {d: lax.rem(x + d, side) for d in steps}
    pairs = [y_at[dy] + x_at[dx] for dy, dx in near]
    z_at = {d: lax.rem(z + d, n_plane) for d in planes}

    def plane_peers(dz, visit):
        if dz:
            def both(i, carry):
                for pair in pairs:
                    visit(z_at[dz] * n_core + i, pair)
                return carry

            lax.fori_loop(0, n_core, both, 0)
        else:
            def partners(i, carry):
                for pair in pairs:
                    visit(z * n_core + lax.rem(c + i, n_core), pair)
                return carry

            lax.fori_loop(1, n_core, partners, 0)
            for pair in pairs[:-1]:
                visit(g, pair)

    barrier = pltpu.get_barrier_semaphore()

    def greet(group, pair):
        pl.semaphore_signal(
            barrier, inc=1, device_id={"group": group, "pair": pair}, device_id_type=MESH
        )

    for dz in planes:
        plane_peers(dz, greet)

    def send_plane(dz, send, recv, source_of, target, at):
        def one(group, pair):
            pltpu.make_async_remote_copy(
                src_ref=source_of(group, pair),
                dst_ref=target.at[at],
                send_sem=send,
                recv_sem=recv,
                device_id={"group": group, "pair": pair},
                device_id_type=MESH,
            ).start()

        plane_peers(dz, one)
        if dz == 0:
            pltpu.make_async_copy(source_of(g, r), target.at[at], recv).start()

    def index_of(group, pair):
        return group * n_pair + pair

    def all_here(number, target):
        pltpu.make_async_copy(target, target, recv_sem.at[number]).wait()

    def all_sent(number, target, count):
        part = target.at[pl.ds(0, count)]
        pltpu.make_async_copy(part, part, send_sem.at[number]).wait()

    for load in loads[:3]:
        load.wait()
    own, row = flat_row(owner_ref[...]), flat_row(row_ref[...])
    lane = iota((1, n_own), 1)
    hot = iota((n_dev, n_own), 0) == own
    hot_f = jnp.where(hot, 1.0, 0.0)
    hot_b = hot_f.astype(bf16)
    before = jnp.where(iota((n_own, n_own), 0) < iota((n_own, n_own), 1), 1.0, 0.0).astype(bf16)
    seen = dot(hot_b, before, 1, 0)
    slot = jnp.sum(hot_f * seen, axis=0, keepdims=True).astype(i32)
    at_slot = iota((slots, n_own), 0) == slot + r * cap
    high = ((row >> 4) + 1).astype(f32)
    low = ((row & 15) * 16 + lane // cand).astype(f32)
    req = dot(hot_b, jnp.where(at_slot, high, 0.0).astype(bf16), 1, 1) * 256.0 + dot(
        hot_b, jnp.where(at_slot, low, 0.0).astype(bf16), 1, 1
    )
    req_out[:, 0, :] = req
    tag = (own * cap + slot).astype(f32)
    for q in range(q_rows):
        key_out[q, :, 0:cand] = tag[:, q * cand : (q + 1) * cand]
        key_out[q, :, cand : 2 * cand] = teach_ref[q : q + 1, :]

    loads[3].wait()
    loads[4].wait()
    pq_own[...] = (dot(q_ref[...], proj[...], 1, 1) * inv_root).astype(bf16)

    pl.semaphore_wait(barrier, n_dev - 1)

    partner = lax.rem(c + 1, n_core)
    there = {"group": z * n_core + partner, "pair": r}

    few = q_all.at[pl.ds(0, n_plane)]

    def spread_rows(source, target, first, second):
        def send(what, group, sem, where):
            pltpu.make_async_remote_copy(
                src_ref=what,
                dst_ref=target.at[group],
                send_sem=send_sem.at[sem],
                recv_sem=recv_sem.at[sem],
                device_id=where,
                device_id_type=MESH,
            ).start()

        for dz in planes[:-1]:
            send(source, g, first, {"group": z_at[dz] * n_core + c, "pair": r})
        send(source, g, second, there)
        pltpu.make_async_copy(source, target.at[g], recv_sem.at[first]).start()

        def forward():
            pltpu.make_async_copy(few, few, recv_sem.at[first]).wait()
            for dz in planes[:-1]:
                group = z_at[dz] * n_core + c
                send(target.at[group], group, second, there)

        return forward

    forward_pq = spread_rows(pq_own, pq_all, 0, 7)
    for dz in planes:
        send_plane(dz, send_sem.at[1], recv_sem.at[1], lambda *p: req_out.at[index_of(*p)], req_in, me)

    def send_key(i, carry):
        other = lax.rem(r + i, n_pair)
        pltpu.make_async_remote_copy(
            src_ref=key_out.at[other],
            dst_ref=key_in.at[r],
            send_sem=send_sem.at[2],
            recv_sem=recv_sem.at[2],
            device_id={"group": g, "pair": other},
            device_id_type=MESH,
        ).start()
        return carry

    lax.fori_loop(1, n_pair, send_key, 0, unroll=True)
    pltpu.make_async_copy(key_out.at[r], key_in.at[r], recv_sem.at[2]).start()

    forward_pq()

    pltpu.make_async_copy(few, few, recv_sem.at[7]).wait()
    loads[5].wait()
    queries_n = n_group * q_rows
    pq = pq_all[...].reshape(queries_n, width)
    s_t = dot(pq, hid[...], 1, 1)
    s_hi[...], s_lo[...] = halves(s_t)

    all_here(1, req_in)
    of_group = iota((1, s_plane), 1) // slots
    for n, dz in enumerate(planes):
        asked = req_in[pl.ds(z_at[dz] * in_plane, in_plane)].reshape(n_core, n_pair, 1, slots)
        asked = jnp.sum(asked, axis=1).astype(i32)
        here = jnp.concatenate([asked[i] for i in range(n_core)], axis=1)
        wanted = jnp.broadcast_to((here >> 4) - 16, (16, s_plane)).astype(jnp.int16)
        wanted = jnp.broadcast_to(wanted[None], (rows // 16, 16, s_plane)).reshape(rows, s_plane)
        mark = jnp.where(iota((rows, s_plane), 0).astype(jnp.int16) == wanted, bf16(1.0), bf16(0.0))
        place[n] = mark
        of_plane = pl.ds(pl.multiple_of(z_at[dz] * q_plane, q_plane), q_plane)
        picks = dot(jnp.concatenate([s_hi[of_plane, :], s_lo[of_plane, :]], axis=0), mark, 1, 0)
        picks = picks[:q_plane] + picks[q_plane:]
        of_query = (here & 15) + q_rows * of_group
        value = jnp.sum(
            jnp.where(iota((q_plane, s_plane), 0) == of_query, picks, 0.0), axis=0, keepdims=True
        )
        for i in range(n_core):
            score_out[z_at[dz] * n_core + i] = value[:, i * slots : (i + 1) * slots]
        send_plane(dz, send_sem.at[3], recv_sem.at[3], lambda group, pair: score_out.at[group], score_in, me)

    all_here(2, key_in)
    keys = key_in[:, 0, :]
    tags = flat_row(keys[:, 0:cand]).astype(i32)
    teach = flat_row(keys[:, cand : 2 * cand])
    k_owner = jnp.where(iota((n_dev, k_all), 0) == tags // cap, 1.0, 0.0).astype(bf16)
    k_slot = jnp.where(
        iota((slots, k_all), 0) == tags % cap + cap * (iota((1, k_all), 1) // cand), 1.0, 0.0
    )

    def column(x):
        return jnp.broadcast_to(x, (128, k_all)).T

    blocks = [(j * 128, (j + 1) * 128) for j in range(k_all // 128)]
    t_col = column(teach)
    t_sum = jnp.concatenate(
        [jnp.sum(jnp.tanh(t_col - teach[:, a:b]), axis=0, keepdims=True) for a, b in blocks], axis=1
    )
    all_here(3, score_in)
    forward_q = spread_rows(q_ref, q_all, 8, 9)
    t_hi, t_lo = halves(score_in[:, 0, :].T)
    picked = dot(jnp.concatenate([t_hi, t_lo], axis=0), k_owner, 1, 0)
    s_k = jnp.sum((picked[:slots] + picked[slots:]) * k_slot, axis=0, keepdims=True)
    s_col = column(s_k)
    sums, slope_sums = [], []
    for a, b in blocks:
        soft = jnp.tanh(s_col - s_k[:, a:b])
        slope = 1.0 - soft * soft
        slopes[:, a:b] = slope
        sums.append(jnp.sum(soft, axis=0, keepdims=True))
        slope_sums.append(jnp.sum(slope, axis=0, keepdims=True))
    gap = 0.5 * (jnp.concatenate(sums, axis=1) - t_sum)
    loss_ref[...] = jnp.broadcast_to(6.0 * jnp.sum(gap * gap, axis=1, keepdims=True) / den, (1, 128))
    grad = gap * (loss_scale * 12.0 / den)
    g_col = column(grad)
    parts = [jnp.sum(g_col * slopes[:, a:b], axis=0, keepdims=True) for a, b in blocks]
    s_grad = 0.5 * (jnp.concatenate(parts, axis=1) - grad * jnp.concatenate(slope_sums, axis=1))
    value_out[:, 0, :] = dot(k_owner, (k_slot * s_grad).astype(bf16), 1, 1)
    for dz in planes:
        send_plane(
            dz, send_sem.at[4], plane_sem.at[(n_plane - dz) % n_plane],
            lambda *p: value_out.at[index_of(*p)], value_in, me,
        )

    row_of = iota((in_plane, slots), 0) // n_pair
    for n, dz in reversed(list(enumerate(planes))):
        arrived = value_in.at[pl.ds(z_at[dz] * in_plane, in_plane)]
        pltpu.make_async_copy(arrived, arrived, plane_sem.at[dz]).wait()
        back = value_in[pl.ds(z_at[dz] * in_plane, in_plane), 0, :]
        spread = jnp.concatenate([jnp.where(row_of == i, back, 0.0) for i in range(n_core)], axis=1)
        of_plane = pl.ds(pl.multiple_of(z_at[dz] * q_plane, q_plane), q_plane)
        w_ref[of_plane, :] = dot(spread.astype(bf16), place[n], 1, 1).astype(bf16)
    per = width // n_dev
    n_b = width // 128
    width_group = n_pair * per
    width_plane = n_core * width_group
    for plane in range(n_plane):
        u = dot(w_ref[...], hid[:, plane * width_plane : (plane + 1) * width_plane], 1, 0)
        by_group = u.reshape(n_plane, n_core, q_rows, width_plane)
        for core in range(n_core):
            columns = u[:, core * width_group : (core + 1) * width_group]
            u_wide[core, plane * n_pair : (plane + 1) * n_pair, n_b:, :] = columns.T.reshape(n_pair, per, n_dev)
            for i in range(width_plane // 128):
                b = plane * (width_plane // 128) + i
                u_wide[core, :, b, :] = by_group[:, core, :, i * 128 : (i + 1) * 128].reshape(half, 128)

    u_there[...] = u_wide[partner].astype(bf16)
    to_partner = pltpu.make_async_remote_copy(
        src_ref=u_there,
        dst_ref=u_here,
        send_sem=send_sem.at[6],
        recv_sem=recv_sem.at[6],
        device_id=there,
        device_id_type=MESH,
    )
    to_partner.start()
    to_partner.wait_recv()
    u_out[...] = (u_wide[c] + u_here[...].astype(f32)).astype(bf16)
    at = z * n_pair + r

    def send_u(plane, pair):
        pltpu.make_async_remote_copy(
            src_ref=u_out.at[plane * n_pair + pair],
            dst_ref=u_in.at[at],
            send_sem=send_sem.at[5],
            recv_sem=recv_sem.at[5],
            device_id={"group": plane * n_core + c, "pair": pair},
            device_id_type=MESH,
        ).start()

    for dz in planes:
        for pair in pairs if dz else pairs[:-1]:
            send_u(z_at[dz], pair)
    pltpu.make_async_copy(u_out.at[at], u_in.at[at], recv_sem.at[5]).start()
    forward_q()
    w_t = w_ref[...].T
    tile = 256
    for i in range(rows // tile):
        hg_ref[i * tile : (i + 1) * tile, :] = dot(w_t[i * tile : (i + 1) * tile], pq, 1, 0).astype(bf16)
    pltpu.make_async_copy(few, few, recv_sem.at[9]).wait()
    q_out[...] = q_all[...].reshape(queries_n, width)
    all_here(5, u_in)
    total_ref[...] = jnp.sum(u_in[...].astype(f32), axis=0) * inv_root

    all_sent(0, q_all, n_plane - 1)
    all_sent(7, q_all, n_plane)
    all_sent(8, q_all, n_plane - 1)
    all_sent(9, q_all, n_plane)
    all_sent(1, req_in, n_dev - 1)
    all_sent(2, key_in, n_pair - 1)
    all_sent(3, score_in, n_dev - 1)
    all_sent(4, value_in, n_dev - 1)
    all_sent(5, u_in, half - 1)
    to_partner.wait_send()


def finish_kernel(
    parts, hg_ref, loss_ref, total_ref, proj, queries, hg_out, loss_out, qg_out, pg_out,
    loss_one, qg_ref, pg_ref, sem,
):
    tile = hg_ref.shape[0] // parts
    stores = [
        pltpu.make_async_copy(
            hg_ref.at[pl.ds(i * tile, tile)], hg_out.at[pl.ds(i * tile, tile)], sem.at[i]
        )
        for i in range(parts)
    ]
    for store in stores:
        store.start()
    loss_one[...] = loss_ref[:, 0:1]
    n_b = proj.shape[0] // 128
    u_row, u_col = total_ref[:n_b], total_ref[n_b:]
    wide = jnp.concatenate(
        [jnp.where(iota((n_b, 128), 0) == b, u_row, 0.0) for b in range(n_b)], axis=1
    )
    w_hi, w_lo = halves(wide)
    query_grad = dot(jnp.concatenate([w_hi, w_lo], axis=0), proj[...], 1, 0)
    qg_ref[...] = jnp.sum(query_grad, axis=0, keepdims=True)
    c_hi, c_lo = halves(u_col)
    proj_grad = dot(jnp.concatenate([c_hi, c_lo], axis=0), queries[...], 1, 0)
    per = pg_ref.shape[0]
    pg_ref[...] = proj_grad[:per] + proj_grad[per:]
    for n, (source, target) in enumerate([(loss_one, loss_out), (qg_ref, qg_out), (pg_ref, pg_out)]):
        store = pltpu.make_async_copy(source, target, sem.at[parts + n])
        store.start()
        stores.append(store)
    for store in stores:
        store.wait()


def shards(query_embed, teacher_scores, pair_owner, pair_row, passage_hidden, projection):
    width = query_embed.shape[2]
    q_rows = query_embed.shape[1]
    cand = teacher_scores.shape[3]
    n_pair, n_group = lax.axis_size("pair"), lax.axis_size("group")
    n_dev = n_pair * n_group
    cap = max(2, 2 * q_rows * cand // n_dev)
    slots = n_pair * cap
    k_all = cand * n_pair
    queries_n = n_group * q_rows
    n_core, side = 2, math.isqrt(n_pair)
    rows = passage_hidden.shape[0]
    per = width // n_dev
    vmem = pl.BlockSpec(memory_space=pltpu.VMEM)
    hbm = pl.BlockSpec(memory_space=pltpu.HBM)
    message = pltpu.VMEM((n_dev, 1, slots), f32)
    results = pl.pallas_call(
        functools.partial(step_kernel, n_group, n_pair, n_core, side, cap),
        out_shape=(
            pltpu.VMEM((rows, width), bf16),
            pltpu.VMEM((1, 128), f32),
            pltpu.VMEM((16, 128), f32),
            pltpu.VMEM((width, width), bf16),
            pltpu.VMEM((queries_n, width), bf16),
        ),
        in_specs=[hbm] * 6,
        out_specs=(vmem,) * 5,
        scratch_shapes=[
            pltpu.VMEM((q_rows, width), bf16),
            pltpu.VMEM((q_rows, cand), f32),
            pltpu.VMEM((q_rows, cand), i32),
            pltpu.VMEM((q_rows, cand), i32),
            pltpu.VMEM((rows, width), bf16),
            pltpu.VMEM((q_rows, width), bf16),
            pltpu.VMEM((n_group, q_rows, width), bf16),
            pltpu.VMEM((n_group, q_rows, width), bf16),
            message,
            message,
            pltpu.VMEM((q_rows, 1, 128), f32),
            pltpu.VMEM((n_pair, 1, 128), f32),
            pltpu.VMEM((n_group, 1, slots), f32),
            message,
            message,
            message,
            pltpu.VMEM((n_group // n_core, rows, n_core * slots), bf16),
            pltpu.VMEM((k_all, k_all), f32),
            pltpu.VMEM((queries_n, rows), bf16),
            pltpu.VMEM((queries_n, rows), bf16),
            pltpu.VMEM((queries_n, rows), bf16),
            pltpu.VMEM((n_core, n_dev // n_core, 16, 128), f32),
            pltpu.VMEM((n_dev // n_core, 16, 128), bf16),
            pltpu.VMEM((n_dev // n_core, 16, 128), bf16),
            pltpu.VMEM((n_dev // n_core, 16, 128), bf16),
            pltpu.VMEM((n_dev // n_core, 16, 128), bf16),
            pltpu.SemaphoreType.DMA((6,)),
            pltpu.SemaphoreType.DMA((10,)),
            pltpu.SemaphoreType.DMA((10,)),
            pltpu.SemaphoreType.DMA((n_group // n_core,)),
        ],
        compiler_params=pltpu.CompilerParams(
            collective_id=0, has_side_effects=True, vmem_limit_bytes=44 * 2**20
        ),
        name="step",
    )(
        *(
            pltpu.with_memory_space_constraint(x, pltpu.HBM)
            for x in (
                query_embed[0],
                teacher_scores.reshape(q_rows, cand),
                pair_owner.reshape(q_rows, cand),
                pair_row.reshape(q_rows, cand),
                passage_hidden,
                projection,
            )
        )
    )
    parts = 8
    hidden_grad, loss, query_grad, projection_grad = pl.pallas_call(
        functools.partial(finish_kernel, parts),
        out_shape=(
            jax.ShapeDtypeStruct((rows, width), bf16),
            jax.ShapeDtypeStruct((1, 1), f32),
            jax.ShapeDtypeStruct((1, width), f32),
            jax.ShapeDtypeStruct((per, width), f32),
        ),
        in_specs=[vmem] * 5,
        out_specs=(hbm,) * 4,
        scratch_shapes=[
            pltpu.VMEM((1, 1), f32),
            pltpu.VMEM((1, width), f32),
            pltpu.VMEM((per, width), f32),
            pltpu.SemaphoreType.DMA((parts + 3,)),
        ],
        compiler_params=pltpu.CompilerParams(vmem_limit_bytes=4 * 2**20),
        name="finish",
    )(*results)
    return loss, query_grad.reshape(1, 1, width), hidden_grad, projection_grad


def solution(mesh):
    placed = (
        P("group", None, None),
        P("group", "pair", None, None),
        P("group", "pair", None, None, None),
        P("group", "pair", None, None),
        P(("group", "pair"), None),
        P(),
    )
    return jax.shard_map(
        shards,
        mesh=mesh,
        in_specs=placed,
        out_specs=(
            P("group", "pair"),
            P("group", "pair", None),
            P(("group", "pair"), None),
            P(("group", "pair"), None),
        ),
        check_vma=False,
    )
```

```python
import functools
import math

import jax
import jax.numpy as jnp
from jax import lax
from jax.experimental import pallas as pl
from jax.experimental.pallas import tpu as pltpu
from jax.sharding import PartitionSpec as P

MESH = pl.DeviceIdType.MESH
loss_scale = 1024.0
f32, bf16, i32 = jnp.float32, jnp.bfloat16, jnp.int32


def iota(shape, dim):
    return lax.broadcasted_iota(i32, shape, dim)


def dot(a, b, ca, cb):
    return lax.dot_general(a, b, (((ca,), (cb,)), ((), ())), preferred_element_type=f32)


def halves(x):
    high = x.astype(bf16)
    return high, (x - high.astype(f32)).astype(bf16)


def flat_row(x):
    return jnp.concatenate([x[i : i + 1, :] for i in range(x.shape[0])], axis=1)


def step_kernel(
    n_group, n_pair, n_core, side, cap,
    q_hbm, teach_hbm, owner_hbm, row_hbm, hid_hbm, proj_hbm,
    hg_ref, loss_ref, total_ref, proj, q_out,
    q_ref, teach_ref, owner_ref, row_ref,
    hid, pq_own, pq_all, q_all, req_out, req_in, key_out, key_in, score_out, score_in,
    value_out, value_in, place, slopes, s_hi, s_lo, w_ref, u_wide, u_there, u_here, u_out, u_in,
    load_sem, send_sem, recv_sem, plane_sem, pair_send, pair_recv,
):
    n_dev = n_group * n_pair
    q_rows, width = q_ref.shape
    cand = teach_ref.shape[1]
    n_own = q_rows * cand
    k_all = cand * n_pair
    slots = n_pair * cap
    rows = hid.shape[0]
    den = float(k_all * (k_all * k_all - 1))
    inv_root = 1.0 / math.sqrt(width)
    g, r = lax.axis_index("group"), lax.axis_index("pair")
    me = g * n_pair + r
    n_plane = n_group // n_core
    in_plane = n_core * n_pair
    q_plane = n_core * q_rows
    s_plane = n_core * slots
    half = n_dev // n_core

    loads = [
        pltpu.make_async_copy(source, target, load_sem.at[n])
        for n, (source, target) in enumerate(
            [(owner_hbm, owner_ref), (row_hbm, row_ref), (teach_hbm, teach_ref), (q_hbm, q_ref),
             (proj_hbm, proj), (hid_hbm, hid)]
        )
    ]
    for load in loads:
        load.start()

    z, c = g // n_core, lax.rem(g, n_core)
    y, x = r // side, lax.rem(r, side)
    planes = sorted(range(n_plane), key=lambda d: -min(d, n_plane - d))
    steps = sorted(range(side), key=lambda d: -min(d, side - d))
    near = [(dy, dx) for dy in steps for dx in steps]
    near.sort(key=lambda d: -sum(min(v, side - v) for v in d))
    y_at = {d: lax.rem(y + d, side) * side for d in steps}
    x_at = {d: lax.rem(x + d, side) for d in steps}
    pairs = [y_at[dy] + x_at[dx] for dy, dx in near]
    z_at = {d: lax.rem(z + d, n_plane) for d in planes}

    def plane_peers(dz, visit):
        if dz:
            def both(i, carry):
                for pair in pairs:
                    visit(z_at[dz] * n_core + i, pair)
                return carry

            lax.fori_loop(0, n_core, both, 0)
        else:
            def partners(i, carry):
                for pair in pairs:
                    visit(z * n_core + lax.rem(c + i, n_core), pair)
                return carry

            lax.fori_loop(1, n_core, partners, 0)
            for pair in pairs[:-1]:
                visit(g, pair)

    barrier = pltpu.get_barrier_semaphore()

    def greet(group, pair):
        pl.semaphore_signal(
            barrier, inc=1, device_id={"group": group, "pair": pair}, device_id_type=MESH
        )

    for dz in planes:
        plane_peers(dz, greet)

    def send_plane(dz, send, recv, source_of, target, at):
        def one(group, pair):
            pltpu.make_async_remote_copy(
                src_ref=source_of(group, pair),
                dst_ref=target.at[at],
                send_sem=send,
                recv_sem=recv,
                device_id={"group": group, "pair": pair},
                device_id_type=MESH,
            ).start()

        plane_peers(dz, one)
        if dz == 0:
            pltpu.make_async_copy(source_of(g, r), target.at[at], recv).start()

    def index_of(group, pair):
        return group * n_pair + pair

    def all_here(number, target):
        pltpu.make_async_copy(target, target, recv_sem.at[number]).wait()

    def all_sent(number, target, count):
        part = target.at[pl.ds(0, count)]
        pltpu.make_async_copy(part, part, send_sem.at[number]).wait()

    for load in loads[:3]:
        load.wait()
    own, row = flat_row(owner_ref[...]), flat_row(row_ref[...])
    lane = iota((1, n_own), 1)
    hot = iota((n_dev, n_own), 0) == own
    hot_f = jnp.where(hot, 1.0, 0.0)
    hot_b = hot_f.astype(bf16)
    before = jnp.where(iota((n_own, n_own), 0) < iota((n_own, n_own), 1), 1.0, 0.0).astype(bf16)
    seen = dot(hot_b, before, 1, 0)
    slot = jnp.sum(hot_f * seen, axis=0, keepdims=True).astype(i32)
    at_slot = iota((slots, n_own), 0) == slot + r * cap
    high = ((row >> 4) + 1).astype(f32)
    low = ((row & 15) * 16 + lane // cand).astype(f32)
    req = dot(hot_b, jnp.where(at_slot, high, 0.0).astype(bf16), 1, 1) * 256.0 + dot(
        hot_b, jnp.where(at_slot, low, 0.0).astype(bf16), 1, 1
    )
    req_out[:, 0, :] = req
    tag = (own * cap + slot).astype(f32)
    for q in range(q_rows):
        key_out[q, :, 0:cand] = tag[:, q * cand : (q + 1) * cand]
        key_out[q, :, cand : 2 * cand] = teach_ref[q : q + 1, :]

    loads[3].wait()
    loads[4].wait()
    pq_own[...] = (dot(q_ref[...], proj[...], 1, 1) * inv_root).astype(bf16)

    pl.semaphore_wait(barrier, n_dev - 1)

    partner = lax.rem(c + 1, n_core)
    there = {"group": z * n_core + partner, "pair": r}

    few = q_all.at[pl.ds(0, n_plane)]

    def spread_rows(source, target, first, second):
        def send(what, group, sem, where):
            pltpu.make_async_remote_copy(
                src_ref=what,
                dst_ref=target.at[group],
                send_sem=send_sem.at[sem],
                recv_sem=recv_sem.at[sem],
                device_id=where,
                device_id_type=MESH,
            ).start()

        for dz in planes[:-1]:
            send(source, g, first, {"group": z_at[dz] * n_core + c, "pair": r})
        send(source, g, second, there)
        pltpu.make_async_copy(source, target.at[g], recv_sem.at[first]).start()

        def forward():
            pltpu.make_async_copy(few, few, recv_sem.at[first]).wait()
            for dz in planes[:-1]:
                group = z_at[dz] * n_core + c
                send(target.at[group], group, second, there)

        return forward

    forward_pq = spread_rows(pq_own, pq_all, 0, 7)
    for dz in planes:
        send_plane(dz, send_sem.at[1], recv_sem.at[1], lambda *p: req_out.at[index_of(*p)], req_in, me)

    def send_key(i, carry):
        other = lax.rem(r + i, n_pair)
        pltpu.make_async_remote_copy(
            src_ref=key_out.at[other],
            dst_ref=key_in.at[r],
            send_sem=send_sem.at[2],
            recv_sem=recv_sem.at[2],
            device_id={"group": g, "pair": other},
            device_id_type=MESH,
        ).start()
        return carry

    lax.fori_loop(1, n_pair, send_key, 0, unroll=True)
    pltpu.make_async_copy(key_out.at[r], key_in.at[r], recv_sem.at[2]).start()

    forward_pq()

    pltpu.make_async_copy(few, few, recv_sem.at[7]).wait()
    loads[5].wait()
    queries_n = n_group * q_rows
    pq = pq_all[...].reshape(queries_n, width)
    s_t = dot(pq, hid[...], 1, 1)
    s_hi[...], s_lo[...] = halves(s_t)

    all_here(1, req_in)
    of_group = iota((1, s_plane), 1) // slots
    for n, dz in enumerate(planes):
        asked = req_in[pl.ds(z_at[dz] * in_plane, in_plane)].reshape(n_core, n_pair, 1, slots)
        asked = jnp.sum(asked, axis=1).astype(i32)
        here = jnp.concatenate([asked[i] for i in range(n_core)], axis=1)
        wanted = jnp.broadcast_to((here >> 4) - 16, (16, s_plane)).astype(jnp.int16)
        wanted = jnp.broadcast_to(wanted[None], (rows // 16, 16, s_plane)).reshape(rows, s_plane)
        mark = jnp.where(iota((rows, s_plane), 0).astype(jnp.int16) == wanted, bf16(1.0), bf16(0.0))
        place[n] = mark
        of_plane = pl.ds(pl.multiple_of(z_at[dz] * q_plane, q_plane), q_plane)
        picks = dot(jnp.concatenate([s_hi[of_plane, :], s_lo[of_plane, :]], axis=0), mark, 1, 0)
        picks = picks[:q_plane] + picks[q_plane:]
        of_query = (here & 15) + q_rows * of_group
        value = jnp.sum(
            jnp.where(iota((q_plane, s_plane), 0) == of_query, picks, 0.0), axis=0, keepdims=True
        )
        for i in range(n_core):
            score_out[z_at[dz] * n_core + i] = value[:, i * slots : (i + 1) * slots]
        send_plane(dz, send_sem.at[3], recv_sem.at[3], lambda group, pair: score_out.at[group], score_in, me)

    all_here(2, key_in)
    keys = key_in[:, 0, :]
    tags = flat_row(keys[:, 0:cand]).astype(i32)
    teach = flat_row(keys[:, cand : 2 * cand])
    k_owner = jnp.where(iota((n_dev, k_all), 0) == tags // cap, 1.0, 0.0).astype(bf16)
    k_slot = jnp.where(
        iota((slots, k_all), 0) == tags % cap + cap * (iota((1, k_all), 1) // cand), 1.0, 0.0
    )

    def column(x):
        return jnp.broadcast_to(x, (128, k_all)).T

    blocks = [(j * 128, (j + 1) * 128) for j in range(k_all // 128)]
    t_col = column(teach)
    t_sum = jnp.concatenate(
        [jnp.sum(jnp.tanh(t_col - teach[:, a:b]), axis=0, keepdims=True) for a, b in blocks], axis=1
    )
    all_here(3, score_in)
    forward_q = spread_rows(q_ref, q_all, 8, 9)
    t_hi, t_lo = halves(score_in[:, 0, :].T)
    picked = dot(jnp.concatenate([t_hi, t_lo], axis=0), k_owner, 1, 0)
    s_k = jnp.sum((picked[:slots] + picked[slots:]) * k_slot, axis=0, keepdims=True)
    s_col = column(s_k)
    sums, slope_sums = [], []
    for a, b in blocks:
        soft = jnp.tanh(s_col - s_k[:, a:b])
        slope = 1.0 - soft * soft
        slopes[:, a:b] = slope
        sums.append(jnp.sum(soft, axis=0, keepdims=True))
        slope_sums.append(jnp.sum(slope, axis=0, keepdims=True))
    gap = 0.5 * (jnp.concatenate(sums, axis=1) - t_sum)
    loss_ref[...] = jnp.broadcast_to(6.0 * jnp.sum(gap * gap, axis=1, keepdims=True) / den, (1, 128))
    grad = gap * (loss_scale * 12.0 / den)
    g_col = column(grad)
    parts = [jnp.sum(g_col * slopes[:, a:b], axis=0, keepdims=True) for a, b in blocks]
    s_grad = 0.5 * (jnp.concatenate(parts, axis=1) - grad * jnp.concatenate(slope_sums, axis=1))
    value_out[:, 0, :] = dot(k_owner, (k_slot * s_grad).astype(bf16), 1, 1)
    for dz in planes:
        send_plane(
            dz, send_sem.at[4], plane_sem.at[(n_plane - dz) % n_plane],
            lambda *p: value_out.at[index_of(*p)], value_in, me,
        )

    row_of = iota((in_plane, slots), 0) // n_pair
    for n, dz in reversed(list(enumerate(planes))):
        arrived = value_in.at[pl.ds(z_at[dz] * in_plane, in_plane)]
        pltpu.make_async_copy(arrived, arrived, plane_sem.at[dz]).wait()
        back = value_in[pl.ds(z_at[dz] * in_plane, in_plane), 0, :]
        spread = jnp.concatenate([jnp.where(row_of == i, back, 0.0) for i in range(n_core)], axis=1)
        of_plane = pl.ds(pl.multiple_of(z_at[dz] * q_plane, q_plane), q_plane)
        w_ref[of_plane, :] = dot(spread.astype(bf16), place[n], 1, 1).astype(bf16)
    per = width // n_dev
    n_b = width // 128
    width_group = n_pair * per
    width_plane = n_core * width_group
    for plane in range(n_plane):
        u = dot(w_ref[...], hid[:, plane * width_plane : (plane + 1) * width_plane], 1, 0)
        by_group = u.reshape(n_plane, n_core, q_rows, width_plane)
        for core in range(n_core):
            columns = u[:, core * width_group : (core + 1) * width_group]
            u_wide[core, plane * n_pair : (plane + 1) * n_pair, n_b:, :] = columns.T.reshape(n_pair, per, n_dev)
            for i in range(width_plane // 128):
                b = plane * (width_plane // 128) + i
                u_wide[core, :, b, :] = by_group[:, core, :, i * 128 : (i + 1) * 128].reshape(half, 128)

    passed = {}
    for dz in planes:
        of_plane = pl.ds(z_at[dz] * n_pair, n_pair)
        u_there[of_plane] = u_wide[partner, of_plane].astype(bf16)
        passed[dz] = pltpu.make_async_remote_copy(
            src_ref=u_there.at[of_plane],
            dst_ref=u_here.at[of_plane],
            send_sem=pair_send.at[dz],
            recv_sem=pair_recv.at[dz],
            device_id=there,
            device_id_type=MESH,
        )
        passed[dz].start()
    at = z * n_pair + r

    def send_u(plane, pair):
        pltpu.make_async_remote_copy(
            src_ref=u_out.at[plane * n_pair + pair],
            dst_ref=u_in.at[at],
            send_sem=send_sem.at[5],
            recv_sem=recv_sem.at[5],
            device_id={"group": plane * n_core + c, "pair": pair},
            device_id_type=MESH,
        ).start()

    for dz in planes:
        of_plane = pl.ds(z_at[dz] * n_pair, n_pair)
        passed[dz].wait_recv()
        u_out[of_plane] = (u_wide[c, of_plane] + u_here[of_plane].astype(f32)).astype(bf16)
        for pair in pairs if dz else pairs[:-1]:
            send_u(z_at[dz], pair)
    pltpu.make_async_copy(u_out.at[at], u_in.at[at], recv_sem.at[5]).start()
    forward_q()
    w_t = w_ref[...].T
    tile = 256
    for i in range(rows // tile):
        hg_ref[i * tile : (i + 1) * tile, :] = dot(w_t[i * tile : (i + 1) * tile], pq, 1, 0).astype(bf16)
    pltpu.make_async_copy(few, few, recv_sem.at[9]).wait()
    q_out[...] = q_all[...].reshape(queries_n, width)
    all_here(5, u_in)
    total_ref[...] = jnp.sum(u_in[...].astype(f32), axis=0) * inv_root

    all_sent(0, q_all, n_plane - 1)
    all_sent(7, q_all, n_plane)
    all_sent(8, q_all, n_plane - 1)
    all_sent(9, q_all, n_plane)
    all_sent(1, req_in, n_dev - 1)
    all_sent(2, key_in, n_pair - 1)
    all_sent(3, score_in, n_dev - 1)
    all_sent(4, value_in, n_dev - 1)
    all_sent(5, u_in, half - 1)
    for copy in passed.values():
        copy.wait_send()


def finish_kernel(
    parts, hg_ref, loss_ref, total_ref, proj, queries, hg_out, loss_out, qg_out, pg_out,
    loss_one, qg_ref, pg_ref, sem,
):
    tile = hg_ref.shape[0] // parts
    stores = [
        pltpu.make_async_copy(
            hg_ref.at[pl.ds(i * tile, tile)], hg_out.at[pl.ds(i * tile, tile)], sem.at[i]
        )
        for i in range(parts)
    ]
    for store in stores:
        store.start()
    loss_one[...] = loss_ref[:, 0:1]
    n_b = proj.shape[0] // 128
    u_row, u_col = total_ref[:n_b], total_ref[n_b:]
    wide = jnp.concatenate(
        [jnp.where(iota((n_b, 128), 0) == b, u_row, 0.0) for b in range(n_b)], axis=1
    )
    w_hi, w_lo = halves(wide)
    query_grad = dot(jnp.concatenate([w_hi, w_lo], axis=0), proj[...], 1, 0)
    qg_ref[...] = jnp.sum(query_grad, axis=0, keepdims=True)
    c_hi, c_lo = halves(u_col)
    proj_grad = dot(jnp.concatenate([c_hi, c_lo], axis=0), queries[...], 1, 0)
    per = pg_ref.shape[0]
    pg_ref[...] = proj_grad[:per] + proj_grad[per:]
    for n, (source, target) in enumerate([(loss_one, loss_out), (qg_ref, qg_out), (pg_ref, pg_out)]):
        store = pltpu.make_async_copy(source, target, sem.at[parts + n])
        store.start()
        stores.append(store)
    for store in stores:
        store.wait()


def shards(query_embed, teacher_scores, pair_owner, pair_row, passage_hidden, projection):
    width = query_embed.shape[2]
    q_rows = query_embed.shape[1]
    cand = teacher_scores.shape[3]
    n_pair, n_group = lax.axis_size("pair"), lax.axis_size("group")
    n_dev = n_pair * n_group
    cap = max(2, 2 * q_rows * cand // n_dev)
    slots = n_pair * cap
    k_all = cand * n_pair
    queries_n = n_group * q_rows
    n_core, side = 2, math.isqrt(n_pair)
    rows = passage_hidden.shape[0]
    per = width // n_dev
    vmem = pl.BlockSpec(memory_space=pltpu.VMEM)
    hbm = pl.BlockSpec(memory_space=pltpu.HBM)
    message = pltpu.VMEM((n_dev, 1, slots), f32)
    results = pl.pallas_call(
        functools.partial(step_kernel, n_group, n_pair, n_core, side, cap),
        out_shape=(
            pltpu.VMEM((rows, width), bf16),
            pltpu.VMEM((1, 128), f32),
            pltpu.VMEM((16, 128), f32),
            pltpu.VMEM((width, width), bf16),
            pltpu.VMEM((queries_n, width), bf16),
        ),
        in_specs=[hbm] * 6,
        out_specs=(vmem,) * 5,
        scratch_shapes=[
            pltpu.VMEM((q_rows, width), bf16),
            pltpu.VMEM((q_rows, cand), f32),
            pltpu.VMEM((q_rows, cand), i32),
            pltpu.VMEM((q_rows, cand), i32),
            pltpu.VMEM((rows, width), bf16),
            pltpu.VMEM((q_rows, width), bf16),
            pltpu.VMEM((n_group, q_rows, width), bf16),
            pltpu.VMEM((n_group, q_rows, width), bf16),
            message,
            message,
            pltpu.VMEM((q_rows, 1, 128), f32),
            pltpu.VMEM((n_pair, 1, 128), f32),
            pltpu.VMEM((n_group, 1, slots), f32),
            message,
            message,
            message,
            pltpu.VMEM((n_group // n_core, rows, n_core * slots), bf16),
            pltpu.VMEM((k_all, k_all), f32),
            pltpu.VMEM((queries_n, rows), bf16),
            pltpu.VMEM((queries_n, rows), bf16),
            pltpu.VMEM((queries_n, rows), bf16),
            pltpu.VMEM((n_core, n_dev // n_core, 16, 128), f32),
            pltpu.VMEM((n_dev // n_core, 16, 128), bf16),
            pltpu.VMEM((n_dev // n_core, 16, 128), bf16),
            pltpu.VMEM((n_dev // n_core, 16, 128), bf16),
            pltpu.VMEM((n_dev // n_core, 16, 128), bf16),
            pltpu.SemaphoreType.DMA((6,)),
            pltpu.SemaphoreType.DMA((10,)),
            pltpu.SemaphoreType.DMA((10,)),
            pltpu.SemaphoreType.DMA((n_group // n_core,)),
            pltpu.SemaphoreType.DMA((n_group // n_core,)),
            pltpu.SemaphoreType.DMA((n_group // n_core,)),
        ],
        compiler_params=pltpu.CompilerParams(
            collective_id=0, has_side_effects=True, vmem_limit_bytes=44 * 2**20
        ),
        name="step",
    )(
        *(
            pltpu.with_memory_space_constraint(x, pltpu.HBM)
            for x in (
                query_embed[0],
                teacher_scores.reshape(q_rows, cand),
                pair_owner.reshape(q_rows, cand),
                pair_row.reshape(q_rows, cand),
                passage_hidden,
                projection,
            )
        )
    )
    parts = 8
    hidden_grad, loss, query_grad, projection_grad = pl.pallas_call(
        functools.partial(finish_kernel, parts),
        out_shape=(
            jax.ShapeDtypeStruct((rows, width), bf16),
            jax.ShapeDtypeStruct((1, 1), f32),
            jax.ShapeDtypeStruct((1, width), f32),
            jax.ShapeDtypeStruct((per, width), f32),
        ),
        in_specs=[vmem] * 5,
        out_specs=(hbm,) * 4,
        scratch_shapes=[
            pltpu.VMEM((1, 1), f32),
            pltpu.VMEM((1, width), f32),
            pltpu.VMEM((per, width), f32),
            pltpu.SemaphoreType.DMA((parts + 3,)),
        ],
        compiler_params=pltpu.CompilerParams(vmem_limit_bytes=4 * 2**20),
        name="finish",
    )(*results)
    return loss, query_grad.reshape(1, 1, width), hidden_grad, projection_grad


def solution(mesh):
    placed = (
        P("group", None, None),
        P("group", "pair", None, None),
        P("group", "pair", None, None, None),
        P("group", "pair", None, None),
        P(("group", "pair"), None),
        P(),
    )
    return jax.shard_map(
        shards,
        mesh=mesh,
        in_specs=placed,
        out_specs=(
            P("group", "pair"),
            P("group", "pair", None),
            P(("group", "pair"), None),
            P(("group", "pair"), None),
        ),
        check_vma=False,
    )
```

```python
import functools
import math

import jax
import jax.numpy as jnp
from jax import lax
from jax.experimental import pallas as pl
from jax.experimental.pallas import tpu as pltpu
from jax.sharding import PartitionSpec as P

MESH = pl.DeviceIdType.MESH
loss_scale = 1024.0
f32, bf16, i32 = jnp.float32, jnp.bfloat16, jnp.int32


def iota(shape, dim):
    return lax.broadcasted_iota(i32, shape, dim)


def dot(a, b, ca, cb):
    return lax.dot_general(a, b, (((ca,), (cb,)), ((), ())), preferred_element_type=f32)


def halves(x):
    high = x.astype(bf16)
    return high, (x - high.astype(f32)).astype(bf16)


def flat_row(x):
    return jnp.concatenate([x[i : i + 1, :] for i in range(x.shape[0])], axis=1)


def step_kernel(
    n_group, n_pair, n_core, side, cap,
    q_hbm, teach_hbm, owner_hbm, row_hbm, hid_hbm, proj_hbm,
    hg_ref, loss_ref, total_ref, proj, q_out,
    q_ref, teach_ref, owner_ref, row_ref,
    hid, pq_own, pq_all, q_all, req_out, req_in, key_out, key_in, score_out, score_in,
    value_out, value_in, place, slopes, s_hi, s_lo, w_ref, u_wide, u_there, u_here, u_out, u_in,
    load_sem, send_sem, recv_sem, plane_sem, pair_send, pair_recv,
):
    n_dev = n_group * n_pair
    q_rows, width = q_ref.shape
    cand = teach_ref.shape[1]
    n_own = q_rows * cand
    k_all = cand * n_pair
    slots = n_pair * cap
    rows = hid.shape[0]
    den = float(k_all * (k_all * k_all - 1))
    inv_root = 1.0 / math.sqrt(width)
    g, r = lax.axis_index("group"), lax.axis_index("pair")
    me = g * n_pair + r
    n_plane = n_group // n_core
    in_plane = n_core * n_pair
    q_plane = n_core * q_rows
    s_plane = n_core * slots
    half = n_dev // n_core

    loads = [
        pltpu.make_async_copy(source, target, load_sem.at[n])
        for n, (source, target) in enumerate(
            [(owner_hbm, owner_ref), (row_hbm, row_ref), (teach_hbm, teach_ref), (q_hbm, q_ref),
             (proj_hbm, proj), (hid_hbm, hid)]
        )
    ]

    z, c = g // n_core, lax.rem(g, n_core)
    y, x = r // side, lax.rem(r, side)
    planes = sorted(range(n_plane), key=lambda d: -min(d, n_plane - d))
    steps = sorted(range(side), key=lambda d: -min(d, side - d))
    near = [(dy, dx) for dy in steps for dx in steps]
    near.sort(key=lambda d: -sum(min(v, side - v) for v in d))
    y_at = {d: lax.rem(y + d, side) * side for d in steps}
    x_at = {d: lax.rem(x + d, side) for d in steps}
    pairs = [y_at[dy] + x_at[dx] for dy, dx in near]
    z_at = {d: lax.rem(z + d, n_plane) for d in planes}

    def plane_peers(dz, visit):
        if dz:
            def both(i, carry):
                for pair in pairs:
                    visit(z_at[dz] * n_core + i, pair)
                return carry

            lax.fori_loop(0, n_core, both, 0)
        else:
            def partners(i, carry):
                for pair in pairs:
                    visit(z * n_core + lax.rem(c + i, n_core), pair)
                return carry

            lax.fori_loop(1, n_core, partners, 0)
            for pair in pairs[:-1]:
                visit(g, pair)

    barrier = pltpu.get_barrier_semaphore()

    def greet(group, pair):
        pl.semaphore_signal(
            barrier, inc=1, device_id={"group": group, "pair": pair}, device_id_type=MESH
        )

    plane_peers(planes[0], greet)
    for load in loads:
        load.start()
    for dz in planes[1:]:
        plane_peers(dz, greet)

    def send_plane(dz, send, recv, source_of, target, at):
        def one(group, pair):
            pltpu.make_async_remote_copy(
                src_ref=source_of(group, pair),
                dst_ref=target.at[at],
                send_sem=send,
                recv_sem=recv,
                device_id={"group": group, "pair": pair},
                device_id_type=MESH,
            ).start()

        plane_peers(dz, one)
        if dz == 0:
            pltpu.make_async_copy(source_of(g, r), target.at[at], recv).start()

    def index_of(group, pair):
        return group * n_pair + pair

    def all_here(number, target):
        pltpu.make_async_copy(target, target, recv_sem.at[number]).wait()

    def all_sent(number, target, count):
        part = target.at[pl.ds(0, count)]
        pltpu.make_async_copy(part, part, send_sem.at[number]).wait()

    for load in loads[:3]:
        load.wait()
    own, row = flat_row(owner_ref[...]), flat_row(row_ref[...])
    lane = iota((1, n_own), 1)
    hot = iota((n_dev, n_own), 0) == own
    hot_f = jnp.where(hot, 1.0, 0.0)
    hot_b = hot_f.astype(bf16)
    before = jnp.where(iota((n_own, n_own), 0) < iota((n_own, n_own), 1), 1.0, 0.0).astype(bf16)
    seen = dot(hot_b, before, 1, 0)
    slot = jnp.sum(hot_f * seen, axis=0, keepdims=True).astype(i32)
    at_slot = iota((slots, n_own), 0) == slot + r * cap
    high = ((row >> 4) + 1).astype(f32)
    low = ((row & 15) * 16 + lane // cand).astype(f32)
    req = dot(hot_b, jnp.where(at_slot, high, 0.0).astype(bf16), 1, 1) * 256.0 + dot(
        hot_b, jnp.where(at_slot, low, 0.0).astype(bf16), 1, 1
    )
    req_out[:, 0, :] = req
    tag = (own * cap + slot).astype(f32)
    for q in range(q_rows):
        key_out[q, :, 0:cand] = tag[:, q * cand : (q + 1) * cand]
        key_out[q, :, cand : 2 * cand] = teach_ref[q : q + 1, :]

    loads[3].wait()
    loads[4].wait()
    pq_own[...] = (dot(q_ref[...], proj[...], 1, 1) * inv_root).astype(bf16)

    pl.semaphore_wait(barrier, n_dev - 1)

    partner = lax.rem(c + 1, n_core)
    there = {"group": z * n_core + partner, "pair": r}

    few = q_all.at[pl.ds(0, n_plane)]

    def spread_rows(source, target, first, second):
        def send(what, group, sem, where):
            pltpu.make_async_remote_copy(
                src_ref=what,
                dst_ref=target.at[group],
                send_sem=send_sem.at[sem],
                recv_sem=recv_sem.at[sem],
                device_id=where,
                device_id_type=MESH,
            ).start()

        for dz in planes[:-1]:
            send(source, g, first, {"group": z_at[dz] * n_core + c, "pair": r})
        send(source, g, second, there)
        pltpu.make_async_copy(source, target.at[g], recv_sem.at[first]).start()

        def forward():
            pltpu.make_async_copy(few, few, recv_sem.at[first]).wait()
            for dz in planes[:-1]:
                group = z_at[dz] * n_core + c
                send(target.at[group], group, second, there)

        return forward

    forward_pq = spread_rows(pq_own, pq_all, 0, 7)
    for dz in planes:
        send_plane(dz, send_sem.at[1], recv_sem.at[1], lambda *p: req_out.at[index_of(*p)], req_in, me)

    def send_key(i, carry):
        other = lax.rem(r + i, n_pair)
        pltpu.make_async_remote_copy(
            src_ref=key_out.at[other],
            dst_ref=key_in.at[r],
            send_sem=send_sem.at[2],
            recv_sem=recv_sem.at[2],
            device_id={"group": g, "pair": other},
            device_id_type=MESH,
        ).start()
        return carry

    lax.fori_loop(1, n_pair, send_key, 0, unroll=True)
    pltpu.make_async_copy(key_out.at[r], key_in.at[r], recv_sem.at[2]).start()

    forward_pq()

    pltpu.make_async_copy(few, few, recv_sem.at[7]).wait()
    loads[5].wait()
    queries_n = n_group * q_rows
    pq = pq_all[...].reshape(queries_n, width)
    s_t = dot(pq, hid[...], 1, 1)
    s_hi[...], s_lo[...] = halves(s_t)

    all_here(1, req_in)
    of_group = iota((1, s_plane), 1) // slots
    for n, dz in enumerate(planes):
        asked = req_in[pl.ds(z_at[dz] * in_plane, in_plane)].reshape(n_core, n_pair, 1, slots)
        asked = jnp.sum(asked, axis=1).astype(i32)
        here = jnp.concatenate([asked[i] for i in range(n_core)], axis=1)
        wanted = jnp.broadcast_to((here >> 4) - 16, (16, s_plane)).astype(jnp.int16)
        wanted = jnp.broadcast_to(wanted[None], (rows // 16, 16, s_plane)).reshape(rows, s_plane)
        mark = jnp.where(iota((rows, s_plane), 0).astype(jnp.int16) == wanted, bf16(1.0), bf16(0.0))
        place[n] = mark
        of_plane = pl.ds(pl.multiple_of(z_at[dz] * q_plane, q_plane), q_plane)
        picks = dot(jnp.concatenate([s_hi[of_plane, :], s_lo[of_plane, :]], axis=0), mark, 1, 0)
        picks = picks[:q_plane] + picks[q_plane:]
        of_query = (here & 15) + q_rows * of_group
        value = jnp.sum(
            jnp.where(iota((q_plane, s_plane), 0) == of_query, picks, 0.0), axis=0, keepdims=True
        )
        for i in range(n_core):
            score_out[z_at[dz] * n_core + i] = value[:, i * slots : (i + 1) * slots]
        send_plane(dz, send_sem.at[3], recv_sem.at[3], lambda group, pair: score_out.at[group], score_in, me)

    all_here(2, key_in)
    keys = key_in[:, 0, :]
    tags = flat_row(keys[:, 0:cand]).astype(i32)
    teach = flat_row(keys[:, cand : 2 * cand])
    k_owner = jnp.where(iota((n_dev, k_all), 0) == tags // cap, 1.0, 0.0).astype(bf16)
    k_slot = jnp.where(
        iota((slots, k_all), 0) == tags % cap + cap * (iota((1, k_all), 1) // cand), 1.0, 0.0
    )

    def column(x):
        return jnp.broadcast_to(x, (128, k_all)).T

    blocks = [(j * 128, (j + 1) * 128) for j in range(k_all // 128)]
    t_col = column(teach)
    t_sum = jnp.concatenate(
        [jnp.sum(jnp.tanh(t_col - teach[:, a:b]), axis=0, keepdims=True) for a, b in blocks], axis=1
    )
    all_here(3, score_in)
    forward_q = spread_rows(q_ref, q_all, 8, 9)
    t_hi, t_lo = halves(score_in[:, 0, :].T)
    picked = dot(jnp.concatenate([t_hi, t_lo], axis=0), k_owner, 1, 0)
    s_k = jnp.sum((picked[:slots] + picked[slots:]) * k_slot, axis=0, keepdims=True)
    s_col = column(s_k)
    sums, slope_sums = [], []
    for a, b in blocks:
        soft = jnp.tanh(s_col - s_k[:, a:b])
        slope = 1.0 - soft * soft
        slopes[:, a:b] = slope
        sums.append(jnp.sum(soft, axis=0, keepdims=True))
        slope_sums.append(jnp.sum(slope, axis=0, keepdims=True))
    gap = 0.5 * (jnp.concatenate(sums, axis=1) - t_sum)
    loss_ref[...] = jnp.broadcast_to(6.0 * jnp.sum(gap * gap, axis=1, keepdims=True) / den, (1, 128))
    grad = gap * (loss_scale * 12.0 / den)
    g_col = column(grad)
    parts = [jnp.sum(g_col * slopes[:, a:b], axis=0, keepdims=True) for a, b in blocks]
    s_grad = 0.5 * (jnp.concatenate(parts, axis=1) - grad * jnp.concatenate(slope_sums, axis=1))
    value_out[:, 0, :] = dot(k_owner, (k_slot * s_grad).astype(bf16), 1, 1)
    for dz in planes:
        send_plane(
            dz, send_sem.at[4], plane_sem.at[(n_plane - dz) % n_plane],
            lambda *p: value_out.at[index_of(*p)], value_in, me,
        )

    row_of = iota((in_plane, slots), 0) // n_pair
    for n, dz in reversed(list(enumerate(planes))):
        arrived = value_in.at[pl.ds(z_at[dz] * in_plane, in_plane)]
        pltpu.make_async_copy(arrived, arrived, plane_sem.at[dz]).wait()
        back = value_in[pl.ds(z_at[dz] * in_plane, in_plane), 0, :]
        spread = jnp.concatenate([jnp.where(row_of == i, back, 0.0) for i in range(n_core)], axis=1)
        of_plane = pl.ds(pl.multiple_of(z_at[dz] * q_plane, q_plane), q_plane)
        w_ref[of_plane, :] = dot(spread.astype(bf16), place[n], 1, 1).astype(bf16)
    per = width // n_dev
    n_b = width // 128
    width_group = n_pair * per
    width_plane = n_core * width_group
    for plane in range(n_plane):
        u = dot(w_ref[...], hid[:, plane * width_plane : (plane + 1) * width_plane], 1, 0)
        by_group = u.reshape(n_plane, n_core, q_rows, width_plane)
        for core in range(n_core):
            columns = u[:, core * width_group : (core + 1) * width_group]
            u_wide[core, plane * n_pair : (plane + 1) * n_pair, n_b:, :] = columns.T.reshape(n_pair, per, n_dev)
            for i in range(width_plane // 128):
                b = plane * (width_plane // 128) + i
                u_wide[core, :, b, :] = by_group[:, core, :, i * 128 : (i + 1) * 128].reshape(half, 128)

    passed = {}
    for dz in planes:
        of_plane = pl.ds(z_at[dz] * n_pair, n_pair)
        u_there[of_plane] = u_wide[partner, of_plane].astype(bf16)
        passed[dz] = pltpu.make_async_remote_copy(
            src_ref=u_there.at[of_plane],
            dst_ref=u_here.at[of_plane],
            send_sem=pair_send.at[dz],
            recv_sem=pair_recv.at[dz],
            device_id=there,
            device_id_type=MESH,
        )
        passed[dz].start()
    at = z * n_pair + r

    def send_u(plane, pair):
        pltpu.make_async_remote_copy(
            src_ref=u_out.at[plane * n_pair + pair],
            dst_ref=u_in.at[at],
            send_sem=send_sem.at[5],
            recv_sem=recv_sem.at[5],
            device_id={"group": plane * n_core + c, "pair": pair},
            device_id_type=MESH,
        ).start()

    for dz in planes:
        of_plane = pl.ds(z_at[dz] * n_pair, n_pair)
        passed[dz].wait_recv()
        u_out[of_plane] = (u_wide[c, of_plane] + u_here[of_plane].astype(f32)).astype(bf16)
        for pair in pairs if dz else pairs[:-1]:
            send_u(z_at[dz], pair)
    pltpu.make_async_copy(u_out.at[at], u_in.at[at], recv_sem.at[5]).start()
    forward_q()
    w_t = w_ref[...].T
    tile = 256
    for i in range(rows // tile):
        hg_ref[i * tile : (i + 1) * tile, :] = dot(w_t[i * tile : (i + 1) * tile], pq, 1, 0).astype(bf16)
    pltpu.make_async_copy(few, few, recv_sem.at[9]).wait()
    q_out[...] = q_all[...].reshape(queries_n, width)
    all_here(5, u_in)
    total_ref[...] = jnp.sum(u_in[...].astype(f32), axis=0) * inv_root

    all_sent(0, q_all, n_plane - 1)
    all_sent(7, q_all, n_plane)
    all_sent(8, q_all, n_plane - 1)
    all_sent(9, q_all, n_plane)
    all_sent(1, req_in, n_dev - 1)
    all_sent(2, key_in, n_pair - 1)
    all_sent(3, score_in, n_dev - 1)
    all_sent(4, value_in, n_dev - 1)
    all_sent(5, u_in, half - 1)
    for copy in passed.values():
        copy.wait_send()


def finish_kernel(
    parts, hg_ref, loss_ref, total_ref, proj, queries, hg_out, loss_out, qg_out, pg_out,
    loss_one, qg_ref, pg_ref, sem,
):
    tile = hg_ref.shape[0] // parts
    stores = [
        pltpu.make_async_copy(
            hg_ref.at[pl.ds(i * tile, tile)], hg_out.at[pl.ds(i * tile, tile)], sem.at[i]
        )
        for i in range(parts)
    ]
    for store in stores:
        store.start()
    loss_one[...] = loss_ref[:, 0:1]
    n_b = proj.shape[0] // 128
    u_row, u_col = total_ref[:n_b], total_ref[n_b:]
    wide = jnp.concatenate(
        [jnp.where(iota((n_b, 128), 0) == b, u_row, 0.0) for b in range(n_b)], axis=1
    )
    w_hi, w_lo = halves(wide)
    query_grad = dot(jnp.concatenate([w_hi, w_lo], axis=0), proj[...], 1, 0)
    qg_ref[...] = jnp.sum(query_grad, axis=0, keepdims=True)
    c_hi, c_lo = halves(u_col)
    proj_grad = dot(jnp.concatenate([c_hi, c_lo], axis=0), queries[...], 1, 0)
    per = pg_ref.shape[0]
    pg_ref[...] = proj_grad[:per] + proj_grad[per:]
    for n, (source, target) in enumerate([(loss_one, loss_out), (qg_ref, qg_out), (pg_ref, pg_out)]):
        store = pltpu.make_async_copy(source, target, sem.at[parts + n])
        store.start()
        stores.append(store)
    for store in stores:
        store.wait()


def shards(query_embed, teacher_scores, pair_owner, pair_row, passage_hidden, projection):
    width = query_embed.shape[2]
    q_rows = query_embed.shape[1]
    cand = teacher_scores.shape[3]
    n_pair, n_group = lax.axis_size("pair"), lax.axis_size("group")
    n_dev = n_pair * n_group
    cap = max(2, 2 * q_rows * cand // n_dev)
    slots = n_pair * cap
    k_all = cand * n_pair
    queries_n = n_group * q_rows
    n_core, side = 2, math.isqrt(n_pair)
    rows = passage_hidden.shape[0]
    per = width // n_dev
    vmem = pl.BlockSpec(memory_space=pltpu.VMEM)
    hbm = pl.BlockSpec(memory_space=pltpu.HBM)
    message = pltpu.VMEM((n_dev, 1, slots), f32)
    results = pl.pallas_call(
        functools.partial(step_kernel, n_group, n_pair, n_core, side, cap),
        out_shape=(
            pltpu.VMEM((rows, width), bf16),
            pltpu.VMEM((1, 128), f32),
            pltpu.VMEM((16, 128), f32),
            pltpu.VMEM((width, width), bf16),
            pltpu.VMEM((queries_n, width), bf16),
        ),
        in_specs=[hbm] * 6,
        out_specs=(vmem,) * 5,
        scratch_shapes=[
            pltpu.VMEM((q_rows, width), bf16),
            pltpu.VMEM((q_rows, cand), f32),
            pltpu.VMEM((q_rows, cand), i32),
            pltpu.VMEM((q_rows, cand), i32),
            pltpu.VMEM((rows, width), bf16),
            pltpu.VMEM((q_rows, width), bf16),
            pltpu.VMEM((n_group, q_rows, width), bf16),
            pltpu.VMEM((n_group, q_rows, width), bf16),
            message,
            message,
            pltpu.VMEM((q_rows, 1, 128), f32),
            pltpu.VMEM((n_pair, 1, 128), f32),
            pltpu.VMEM((n_group, 1, slots), f32),
            message,
            message,
            message,
            pltpu.VMEM((n_group // n_core, rows, n_core * slots), bf16),
            pltpu.VMEM((k_all, k_all), f32),
            pltpu.VMEM((queries_n, rows), bf16),
            pltpu.VMEM((queries_n, rows), bf16),
            pltpu.VMEM((queries_n, rows), bf16),
            pltpu.VMEM((n_core, n_dev // n_core, 16, 128), f32),
            pltpu.VMEM((n_dev // n_core, 16, 128), bf16),
            pltpu.VMEM((n_dev // n_core, 16, 128), bf16),
            pltpu.VMEM((n_dev // n_core, 16, 128), bf16),
            pltpu.VMEM((n_dev // n_core, 16, 128), bf16),
            pltpu.SemaphoreType.DMA((6,)),
            pltpu.SemaphoreType.DMA((10,)),
            pltpu.SemaphoreType.DMA((10,)),
            pltpu.SemaphoreType.DMA((n_group // n_core,)),
            pltpu.SemaphoreType.DMA((n_group // n_core,)),
            pltpu.SemaphoreType.DMA((n_group // n_core,)),
        ],
        compiler_params=pltpu.CompilerParams(
            collective_id=0, has_side_effects=True, vmem_limit_bytes=44 * 2**20
        ),
        name="step",
    )(
        *(
            pltpu.with_memory_space_constraint(x, pltpu.HBM)
            for x in (
                query_embed[0],
                teacher_scores.reshape(q_rows, cand),
                pair_owner.reshape(q_rows, cand),
                pair_row.reshape(q_rows, cand),
                passage_hidden,
                projection,
            )
        )
    )
    parts = 4
    hidden_grad, loss, query_grad, projection_grad = pl.pallas_call(
        functools.partial(finish_kernel, parts),
        out_shape=(
            jax.ShapeDtypeStruct((rows, width), bf16),
            jax.ShapeDtypeStruct((1, 1), f32),
            jax.ShapeDtypeStruct((1, width), f32),
            jax.ShapeDtypeStruct((per, width), f32),
        ),
        in_specs=[vmem] * 5,
        out_specs=(hbm,) * 4,
        scratch_shapes=[
            pltpu.VMEM((1, 1), f32),
            pltpu.VMEM((1, width), f32),
            pltpu.VMEM((per, width), f32),
            pltpu.SemaphoreType.DMA((parts + 3,)),
        ],
        compiler_params=pltpu.CompilerParams(vmem_limit_bytes=4 * 2**20),
        name="finish",
    )(*results)
    return loss, query_grad.reshape(1, 1, width), hidden_grad, projection_grad


def solution(mesh):
    placed = (
        P("group", None, None),
        P("group", "pair", None, None),
        P("group", "pair", None, None, None),
        P("group", "pair", None, None),
        P(("group", "pair"), None),
        P(),
    )
    return jax.shard_map(
        shards,
        mesh=mesh,
        in_specs=placed,
        out_specs=(
            P("group", "pair"),
            P("group", "pair", None),
            P(("group", "pair"), None),
            P(("group", "pair"), None),
        ),
        check_vma=False,
    )
```
